32 devices in a mesh: pose: 4 (over y, core), slab: 8 (over z, x).
Axes of the slice: x: 2, y: 2, z: 4, core: 2. Of those that a mesh axis runs over, the one named last changes fastest.
Arguments:
- coords: float32 [4, 3, 2048], P('pose'), may hold values from -12 to 12, as said below
- atom_types: int32 [4, 2048], P('pose'), may hold values from 0 to 27
- counts: int32 [4], P('pose'), may hold values from 1024 to 2048, as said below
- labels: int32 [4], P('pose'), may hold values from 0 to 1
- receptor_density: bfloat16 [4, 28, 16, 4096], P('pose', None, 'slab'), may hold values from 0 to 1.5
- type_radii: float32 [28], replicated, may hold values from 1.2 to 2.2
- w_stem: bfloat16 [32, 28, 3, 3, 3], replicated, may hold values from -1.25 to 1.25
- w_one: bfloat16 [32, 32, 3, 3, 3], replicated, may hold values from -0.21875 to 0.21875
- w_two: bfloat16 [32, 32, 3, 3, 3], replicated, may hold values from -0.21875 to 0.21875
- w_head: float32 [32], replicated, may hold values from -8 to 8
Outputs:
- scores: float32 [4], P('pose')
- pose_loss: float32 [4], P('pose')
- atom_grad: float32 [4, 3, 2048], P('pose')
- grad_stem: float32 [32, 28, 3, 3, 3], replicated
- grad_one: float32 [32, 32, 3, 3, 3], replicated
- grad_two: float32 [32, 32, 3, 3, 3], replicated
- grad_head: float32 [32], replicated
The draws below stay inside these ranges and needn't reach their ends.
Inputs may be any that keep to these rules, and one draw needn't show every extreme that they name: The live atoms of a pose are the first counts[p] slots; every pose has 1024 or more of them, and some pose has all 2048. `coords`: every atom lies inside the box of the grid, 0.75 or more from its faces.
All inputs are finite; a program needn't handle non-finite values.
Results may differ from the reference program's by a relative error of at most 0.005.
The reference program's roundings to bfloat16 on the way count: a program that leaves them out, or rounds other values in their place, can miss the bound.
Values may be sent and summed in bfloat16 or wider, within the bound.
No kernel may reach another device: no remote copies, remote signals or barrier semaphores. Data moves between devices by JAX's collectives and lax.ppermute only.
A program may use at most 256 MiB of HBM per device.

```python
import math
import jax
import jax.numpy as jnp
from jax import lax

TYPES = 28
WIDTH = 32
NXY = 64
ATOMS = 2048
NZ = 16
POSES = 4


resolution = 0.375


def draw_coords(key, part):
    subkeys = jax.random.split(key, 2)
    half_xy = 0.5 * NXY * resolution - 0.75
    half_z = 0.5 * NZ * resolution - 0.75
    across = jax.random.uniform(subkeys[0], (POSES, 2, ATOMS), jnp.float32, -half_xy, half_xy)
    growth = 2.0
    fraction = jax.random.uniform(subkeys[1], (POSES, 1, ATOMS), jnp.float32)
    height_frac = (jnp.sqrt(1.0 + 2.0 * growth * fraction * (1.0 + 0.5 * growth)) - 1.0) / growth
    height = -half_z + 2.0 * half_z * height_frac
    return jnp.concatenate([across, height], axis=1)


def draw_counts(key, part):
    subkeys = jax.random.split(key, 2)
    sampled = jax.random.randint(subkeys[0], (POSES,), ATOMS // 2, ATOMS + 1, jnp.int32)
    fullest = jax.random.randint(subkeys[1], (), 0, POSES, jnp.int32)
    return jnp.where(jnp.arange(POSES, dtype=jnp.int32) == fullest, ATOMS, sampled)


def plant(drawn, own_key, least, high):
    extent = drawn.shape
    index_at = [jax.random.randint(jax.random.fold_in(own_key, axis), (), 0, extent[axis]) for axis in range(len(extent))]
    drawn = drawn.at[tuple(index_at)].set(least)
    longest = extent.index(max(extent))
    index_at[longest] = (index_at[longest] + 1) % extent[longest]
    return drawn.at[tuple(index_at)].set(high)


def steps_of(key, shape, shards, least, top_value):
    gain, own = 1.0, jax.random.fold_in(key, 6)
    for dim, shards_of in shards:
        draws = jnp.exp(jax.random.uniform(jax.random.fold_in(own, dim), (shards_of,), jnp.float32, least / len(shards), top_value / len(shards)))
        gain = gain * jnp.repeat(draws, shape[dim] // shards_of).reshape([-1 if axis == dim else 1 for axis in range(len(shape))])
    return gain


def normal_values(stream_key, dims, spread, reach, kind=jnp.bfloat16):
    return jnp.clip(spread * jax.random.normal(stream_key, dims, jnp.float32), -reach, reach).astype(kind)


def setup_inputs(seed: int = 0) -> dict:
    key_of = jax.random.split(jax.random.key(seed), 11)
    coords = draw_coords(jax.random.fold_in(key_of[10], 71), 0)
    atom_types = plant(jax.random.randint(key_of[1], (POSES, ATOMS), 0, TYPES), jax.random.fold_in(key_of[1], 1), 0, TYPES - 1).astype(jnp.int32)
    counts = draw_counts(jax.random.fold_in(key_of[10], 71), 0)
    labels = plant(jax.random.randint(key_of[3], (POSES,), 0, 2), jax.random.fold_in(key_of[3], 1), 0, 1).astype(jnp.int32)
    receptor_density = jnp.clip(1.5 * jax.random.uniform(key_of[4], (POSES, TYPES, NZ, NXY * NXY), jnp.float32) ** steps_of(key_of[4], (POSES, TYPES, NZ, NXY * NXY), ((0, 4), (2, 8)), -0.2, 0.2), 0.0, 1.5).astype(jnp.bfloat16)
    type_radii = jnp.clip(jnp.exp(jax.random.uniform(key_of[5], (TYPES,), jnp.float32, math.log(1.2), math.log(2.2))), 1.2, 2.2)
    w_stem = normal_values(key_of[6], (WIDTH, TYPES, 3, 3, 3), 27 ** -0.5, 1.25)
    w_one = normal_values(key_of[7], (WIDTH, WIDTH, 3, 3, 3), (27 * WIDTH) ** -0.5, 0.21875)
    w_two = normal_values(key_of[8], (WIDTH, WIDTH, 3, 3, 3), (27 * WIDTH) ** -0.5, 0.21875)
    w_head = normal_values(key_of[9], (WIDTH,), 2.0, 8.0, jnp.float32)
    return dict(coords=coords, atom_types=atom_types, counts=counts, labels=labels, receptor_density=receptor_density, type_radii=type_radii, w_stem=w_stem, w_one=w_one, w_two=w_two, w_head=w_head)


resolution = 0.375
highest = lax.Precision.HIGHEST

def gauss_table(centres, places, inv_sq):
    offset = centres[:, None] - places[None, :]
    bumps = jnp.exp(-2.0 * offset * offset * inv_sq[None, :])
    return (bumps, 4.0 * offset * inv_sq[None, :] * bumps)

def conv_same(volume, kernel):
    result = lax.conv_general_dilated(volume[None].astype(jnp.float32), kernel.astype(jnp.float32), (1, 1, 1), [(1, 1), (1, 1), (1, 1)], dimension_numbers=('NCDHW', 'OIDHW', 'NCDHW'), precision=highest)
    return result[0]

def flipped(kernel):
    return jnp.flip(kernel, (2, 3, 4)).transpose(1, 0, 2, 3, 4)

def kernel_grad(volume, upstream):
    padded = jnp.pad(volume.astype(jnp.float32), ((0, 0), (1, 1), (1, 1), (1, 1)))
    upper = upstream.astype(jnp.float32)
    blocks = []
    for depth_off in range(3):
        for row_off in range(3):
            for col_off in range(3):
                window = padded[:, depth_off:depth_off + NZ, row_off:row_off + NXY, col_off:col_off + NXY]
                blocks.append(jnp.einsum('ozxy,izxy->oi', upper, window, precision=highest))
    return jnp.stack(blocks, axis=-1).reshape(upper.shape[0], volume.shape[0], 3, 3, 3)

def pose_pass(coords3, kind_row, live_count, pose_label, receptor, type_radii, w_stem, w_one, w_two, w_head):
    type_count = type_radii.shape[0]
    atom_count = kind_row.shape[0]
    cell_count = NZ * NXY * NXY
    centres_xy = (jnp.arange(NXY, dtype=jnp.float32) + 0.5 - 0.5 * NXY) * resolution
    centres_z = (jnp.arange(NZ, dtype=jnp.float32) + 0.5 - 0.5 * NZ) * resolution
    type_hits = (kind_row[None, :] == jnp.arange(type_count, dtype=jnp.int32)[:, None]).astype(jnp.float32)
    alive = (jnp.arange(atom_count, dtype=jnp.int32) < live_count).astype(jnp.float32)
    live_types = type_hits * alive[None, :]
    radius = lax.optimization_barrier(jnp.sum(type_hits * type_radii[:, None], axis=0))
    inv_sq = 1.0 / (radius * radius)
    gauss_x, slope_x = gauss_table(centres_xy, coords3[0], inv_sq)
    gauss_y, slope_y = gauss_table(centres_xy, coords3[1], inv_sq)
    gauss_z, slope_z = gauss_table(centres_z, coords3[2], inv_sq)
    across_table = (live_types[:, None, :] * gauss_y[None]).reshape(type_count * NXY, atom_count).astype(jnp.bfloat16)
    slope_table = (live_types[:, None, :] * slope_y[None]).reshape(type_count * NXY, atom_count).astype(jnp.bfloat16)
    depth_table = (gauss_z[:, None, :] * gauss_x[None]).reshape(NZ * NXY, atom_count).astype(jnp.bfloat16)
    row_cols = jnp.dot(depth_table.astype(jnp.float32), across_table.astype(jnp.float32).T, preferred_element_type=jnp.float32, precision=highest)
    splat = row_cols.reshape(NZ, NXY, type_count, NXY).transpose(2, 0, 1, 3)
    density = (splat + receptor.astype(jnp.float32).reshape(type_count, NZ, NXY, NXY)).astype(jnp.bfloat16)
    stem_pre = conv_same(density, w_stem)
    hidden_one = jnp.maximum(stem_pre, 0.0).astype(jnp.bfloat16)
    second_pre = conv_same(hidden_one, w_one)
    hidden_two = jnp.maximum(second_pre, 0.0).astype(jnp.bfloat16)
    summed = hidden_one.astype(jnp.float32) + conv_same(hidden_two, w_two)
    pooled = lax.optimization_barrier(jnp.mean(jnp.maximum(summed, 0.0), axis=(1, 2, 3)))
    pose_score = jnp.sum(pooled * w_head)
    label_sign = (2 * pose_label - 1).astype(jnp.float32)
    pose_loss = jax.nn.softplus(-label_sign * pose_score)
    score_grad = -label_sign * jax.nn.sigmoid(-label_sign * pose_score)
    top_grad = jnp.where(summed > 0, (score_grad * w_head)[:, None, None, None], 0.0).astype(jnp.bfloat16)
    grad_two = kernel_grad(hidden_two, top_grad) / cell_count
    mid_grad = jnp.where(second_pre > 0, conv_same(top_grad, flipped(w_two)), 0.0).astype(jnp.bfloat16)
    grad_one = kernel_grad(hidden_one, mid_grad) / cell_count
    back_one = top_grad.astype(jnp.float32) + conv_same(mid_grad, flipped(w_one))
    stem_grad = jnp.where(stem_pre > 0, back_one, 0.0).astype(jnp.bfloat16)
    grad_stem = kernel_grad(density, stem_grad) / cell_count
    density_grad = conv_same(stem_grad, flipped(w_stem)).astype(jnp.bfloat16)
    grid_rows = density_grad.transpose(1, 2, 0, 3).reshape(NZ * NXY, type_count * NXY).astype(jnp.float32)
    rows_plain = jnp.dot(grid_rows, across_table.astype(jnp.float32), preferred_element_type=jnp.float32, precision=highest).reshape(NZ, NXY, atom_count)
    rows_slope = jnp.dot(grid_rows, slope_table.astype(jnp.float32), preferred_element_type=jnp.float32, precision=highest).reshape(NZ, NXY, atom_count)
    along_x = jnp.einsum('zxa,za,xa->a', rows_plain, gauss_z, slope_x, precision=highest)
    along_y = jnp.einsum('zxa,za,xa->a', rows_slope, gauss_z, gauss_x, precision=highest)
    along_z = jnp.einsum('zxa,za,xa->a', rows_plain, slope_z, gauss_x, precision=highest)
    atom_force = jnp.stack([along_x, along_y, along_z])
    return (pose_score, pose_loss, atom_force, grad_stem, grad_one, grad_two, score_grad * pooled)

def reference(coords, atom_types, counts, labels, receptor_density, type_radii, w_stem, w_one, w_two, w_head):

    def single(inputs):
        return pose_pass(inputs[0], inputs[1], inputs[2], inputs[3], inputs[4], type_radii, w_stem, w_one, w_two, w_head)
    results = lax.map(single, (coords, atom_types, counts, labels, receptor_density))
    return (results[0], results[1], results[2], lax.optimization_barrier(jnp.sum(results[3], axis=0)), lax.optimization_barrier(jnp.sum(results[4], axis=0)), lax.optimization_barrier(jnp.sum(results[5], axis=0)), lax.optimization_barrier(jnp.sum(results[6], axis=0)))
```

```python
import functools

import jax
import jax.numpy as jnp
from jax import lax
from jax.experimental import pallas as pl
from jax.experimental.pallas import tpu as pltpu
from jax.sharding import PartitionSpec as P

NXY = 64
resolution = 0.375
f32 = jnp.float32
bf16 = jnp.bfloat16

JB = 16
OWN = 32
RD, RS, R2, R3, RM, RG = 38, 37, 36, 35, 34, 33
BR = 41 * JB
CH = 128
NCH = 5
NT = (((1,), (1,)), ((), ()))
NN = (((1,), (0,)), ((), ()))


def dotf(a, b, dims):
    return lax.dot_general(a, b, dims, preferred_element_type=f32)


def lane_block(shape):
    return lax.broadcasted_iota(jnp.int32, shape, 1) // 32


def spread(block, turn):
    if turn == 1:
        return block
    out = pltpu.roll(block, ((turn - 1) * 32) % 128, 1)
    lanes = lane_block(block.shape)
    if turn == 0:
        return jnp.where(lanes == 3, 0.0, out)
    if turn == 3:
        return jnp.where(lanes == 0, 0.0, out)
    return out


def one_block(block, source, target):
    out = pltpu.roll(block, ((target - source) * 32) % 128, 1)
    return jnp.where(lane_block(block.shape) == target, out, 0.0)


def build_forward(u_ref, conv, flip, w_ref):
    zero = jnp.zeros((32, 128), f32)

    def body(f, carry):
        fe = jnp.where(flip == 0, f, 2 - f)
        for p in range(2):
            for jo in range(4):
                rows = pl.ds(p * 128 + jo * 32, 32)
                for half in range(2):
                    edge = zero
                    for q in (2 * half, 2 * half + 1):
                        e = q - p
                        main = zero
                        if 0 <= e <= 2:
                            u = u_ref[conv * 9 + e * 3 + fe]
                            main = spread(u, jo)
                            if jo == 0:
                                edge = edge + one_block(u, 0, 2 * (q % 2))
                            if jo == 3:
                                edge = edge + one_block(u, 2, 2 * (q % 2) + 1)
                        w_ref[f, rows, pl.ds(q * 128, 128)] = main.astype(bf16)
                    w_ref[f, rows, pl.ds(512 + half * 128, 128)] = edge.astype(bf16)
        return carry

    lax.fori_loop(0, 3, body, 0)


def build_backward(u_ref, conv, flip, w_ref):
    zero = jnp.zeros((32, 128), f32)

    def body(f, carry):
        fe = jnp.where(flip == 0, 2 - f, f)
        for q in range(4):
            for p in range(2):
                e = 2 - (q - p)
                lanes = pl.ds(p * 128, 128)
                ok = 0 <= e <= 2
                u = u_ref[conv * 9 + e * 3 + fe] if ok else None
                for jc in range(4):
                    w_ref[f, pl.ds(q * 128 + jc * 32, 32), lanes] = (spread(u, jc) if ok else zero).astype(bf16)
                low = one_block(u, 2, 0) if ok else zero
                high = one_block(u, 0, 3) if ok else zero
                w_ref[f, pl.ds(512 + q * 64, 32), lanes] = low.astype(bf16)
                w_ref[f, pl.ds(512 + q * 64 + 32, 32), lanes] = high.astype(bf16)
        return carry

    lax.fori_loop(0, 3, body, 0)


def edges(a, b):
    n = a.shape[0]
    lanes = lane_block((n, 128))
    mixed = jnp.where(lanes < 2, pltpu.roll(a, 32, 1), pltpu.roll(b, 96, 1))
    down = pltpu.roll(mixed, 1, 0)
    up = pltpu.roll(mixed, n - 1, 0)
    jb = lax.broadcasted_iota(jnp.int32, (n, 128), 0) % JB
    low = jnp.where(jb == 0, 0.0, down)
    high = jnp.where(jb == JB - 1, 0.0, up)
    return jnp.where(lanes % 2 == 0, low, high)


def patch(x_ref, e_ref, plane, pair, f, n):
    sl = pl.ds(f * JB, n)
    return [x_ref[plane + k, sl, :] for k in range(4)] + [e_ref[pair + k, sl, :] for k in range(2)]


def conv_pair(x_ref, e_ref, plane, pair, rows, w_ref, acc_ref, dims):
    n = rows * JB
    total = None
    for f in range(3):
        lhs = jnp.concatenate(patch(x_ref, e_ref, plane, pair, f, n), axis=1)
        part = dotf(lhs, w_ref[f], dims)
        total = part if total is None else total + part
    acc_ref[pl.ds(0, n), :] = total


def put_pair(main_ref, e_ref, plane, pair, at, va, vb):
    main_ref[plane, pl.ds(at, va.shape[0]), :] = va.astype(bf16)
    main_ref[plane + 1, pl.ds(at, va.shape[0]), :] = vb.astype(bf16)
    if e_ref is not None:
        e_ref[pair, pl.ds(at, va.shape[0]), :] = edges(va, vb).astype(bf16)


def rounded(v):
    return v.astype(bf16).astype(f32)


def clear_pad(ref):
    for k in range(ref.shape[0]):
        ref[k, pl.ds(0, JB), :] = jnp.zeros((JB, 128), ref.dtype)


def pack_kernel(meta, raw_ref, self_ref, part_ref):
    h = meta[1]
    row = lax.broadcasted_iota(jnp.int32, (256, 256), 0)
    col = lax.broadcasted_iota(jnp.int32, (256, 256), 1)
    mask = jnp.where((row // 32) % 4 == col % 4, 1.0, 0.0).astype(bf16)
    srow = lax.broadcasted_iota(jnp.int32, (64, 256), 0)
    scol = lax.broadcasted_iota(jnp.int32, (64, 256), 1)
    same = srow % JB == (scol // 4) % JB
    for v in range(2):
        a = srow // JB if v == 0 else 3 - srow // JB
        pick = jnp.where(same & (scol // 64 == a), 1.0, 0.0).astype(bf16)
        for ch in range(10):
            at = (ch if v == 0 else 15 - ch) * 256
            x0 = raw_ref[0, :, pl.ds(at, 256)]
            x1 = raw_ref[1, :, pl.ds(at, 256)]
            wide = jnp.concatenate([x0] * 4 + [x1] * 4, axis=0) * mask
            out = dotf(pick, wide, NT).astype(bf16)
            n = 64 if ch < 9 else 32
            for p in range(2):
                val = out[:n, p * 128 : (p + 1) * 128]

                @pl.when(h == v)
                def _():
                    self_ref[p, pl.ds(ch * 64, n), :] = val

                @pl.when(h != v)
                def _():
                    part_ref[p, pl.ds(ch * 64, n), :] = val


def atom_terms(meta, radii, types, count_at):
    radius = jnp.zeros(types.shape, f32)
    for c in range(radii.shape[0]):
        radius = radius + jnp.where(types == c, radii[c], 0.0)
    return 1.0 / (radius * radius)


def centre_rows(n, first, step, half):
    row = lax.broadcasted_iota(jnp.int32, (n, 1), 0)
    return ((first + step * row).astype(f32) + 0.5 - half) * resolution


def bump(centre, place, inv_sq):
    offset = centre - place
    return jnp.exp(-2.0 * offset * offset * inv_sq), offset


def first_row(meta):
    return jnp.where(meta[1] == 0, 0, NXY - 1), jnp.where(meta[1] == 0, 1, -1)


def splat_kernel(meta, radii, coords_ref, types_ref, out_ref, z_ref, gy_ref, live_ref, y_ref):
    atoms = types_ref.shape[1]
    types = types_ref[...]
    inv_sq = atom_terms(meta, radii, types, 2)
    top, step = first_row(meta)
    gx = bump(centre_rows(40, top, step, 0.5 * NXY), coords_ref[0:1, :], inv_sq)[0]
    half_z = 0.5 * meta[3].astype(f32)
    gz = bump(centre_rows(16, 4 * meta[0] - 3, 1, half_z), coords_ref[2:3, :], inv_sq)[0]
    for q in range(10):
        z_ref[pl.ds(q * 40, 40), :] = (gz[q : q + 1, :] * gx).astype(bf16)
    gy_ref[...] = bump(centre_rows(NXY, 0, 1, 0.5 * NXY), coords_ref[1:2, :], inv_sq)[0]
    kind = lax.broadcasted_iota(jnp.int32, (32, atoms), 0)
    slot = lax.broadcasted_iota(jnp.int32, (32, atoms), 1)
    live_ref[...] = jnp.where((types == kind) & (slot < meta[2]), 1.0, 0.0)

    def body(step8, carry):
        for t in range(8):
            y = gy_ref[pl.ds(step8 * 8 + t, 1), :]
            y_ref[pl.ds(t * 32, 32), :] = (live_ref[...] * y).astype(bf16)
        out = dotf(z_ref[...], y_ref[...], NT)
        out_ref[pl.ds(2 * step8, 400, stride=JB), :] = out[:, :128]
        out_ref[pl.ds(2 * step8 + 1, 400, stride=JB), :] = out[:, 128:]
        return carry

    lax.fori_loop(0, 8, body, 0)


def forward_kernel(
    meta, splat_ref, lo_ref, own_ref, hi_ref, u_ref,
    x_ref, ex_ref, h1_ref, e1_ref, h2_ref, e2_ref, m3_ref, up_ref, dn_ref, pool_ref,
    w_ref, acc_ref,
):
    first = 4 * meta[0] - 3
    depth = meta[3]
    flip = meta[1]
    for ref in (x_ref, ex_ref, h1_ref, e1_ref, h2_ref, e2_ref):
        clear_pad(ref)

    def inside(q):
        z = first + q
        return jnp.where((z >= 0) & (z < depth), 1.0, 0.0)

    def receptor(q, sl):
        if q < 3:
            return lo_ref[q, sl, :]
        if q < 7:
            return own_ref[q - 3, sl, :]
        return hi_ref[q - 7, sl, :]

    for m in range(5):
        def density(c, carry):
            at = c * 304
            sl = pl.ds(pl.multiple_of(at, 16), 304)
            vals = []
            for q in (2 * m, 2 * m + 1):
                v = splat_ref[pl.ds(pl.multiple_of(q * 640 + at, 16), 304), :] + receptor(q, sl).astype(f32)
                vals.append(rounded(v * inside(q)))
            put_pair(x_ref, ex_ref, 2 * m, m, pl.multiple_of(JB + at, 16), *vals)
            return carry

        lax.fori_loop(0, 2, density, 0)

    build_forward(u_ref, 0, flip, w_ref)

    def stem(m, carry):
        conv_pair(x_ref, ex_ref, 2 * m, m, RS, w_ref, acc_ref, NT)
        ia, ib = inside(2 * m + 1), inside(2 * m + 2)
        for c in range(NCH):
            acc = jnp.maximum(acc_ref[pl.ds(c * CH, CH), :], 0.0)
            put_pair(h1_ref, e1_ref, 2 * m, m, JB + c * CH, rounded(acc[:, :128] * ia), rounded(acc[:, 128:] * ib))
        return carry

    lax.fori_loop(0, 4, stem, 0)
    build_forward(u_ref, 1, flip, w_ref)

    def second(m, carry):
        conv_pair(h1_ref, e1_ref, 2 * m, m, R2, w_ref, acc_ref, NT)
        ia, ib = inside(2 * m + 2), inside(2 * m + 3)
        for c in range(NCH):
            acc = jnp.maximum(acc_ref[pl.ds(c * CH, CH), :], 0.0)
            put_pair(h2_ref, e2_ref, 2 * m, m, JB + c * CH, rounded(acc[:, :128] * ia), rounded(acc[:, 128:] * ib))
        return carry

    lax.fori_loop(0, 3, second, 0)
    build_forward(u_ref, 2, flip, w_ref)

    def third(m, pool):
        conv_pair(h2_ref, e2_ref, 2 * m, m, R3, w_ref, acc_ref, NT)
        for c in range(7):
            sl = pl.ds(c * 80, 80)
            src = pl.ds(JB + c * 80, 80)
            for k in range(2):
                keep = h1_ref[2 * m + 2 + k, src, :].astype(f32)
                summed = keep + acc_ref[sl, pl.ds(128 * k, 128)]
                top = jnp.maximum(summed, 0.0)
                if (c + 1) * 80 > OWN * JB:
                    row = lax.broadcasted_iota(jnp.int32, (80, 128), 0) + c * 80
                    top = jnp.where(row < OWN * JB, top, 0.0)
                pool = pool + jnp.sum(top, axis=0, keepdims=True)
                m3_ref[2 * m + k, sl, :] = jnp.where(summed > 0.0, 1.0, 0.0).astype(bf16)
        return pool

    pool = lax.fori_loop(0, 2, third, jnp.zeros((1, 128), f32))
    pool = pool + pltpu.roll(pool, 64, 1)
    pool = pool + pltpu.roll(pool, 32, 1)
    pool_ref[...] = jnp.broadcast_to(pool, (8, 128))
    for k in range(3):
        up_ref[k] = m3_ref[k + 1]
        dn_ref[k] = m3_ref[k]
    up_ref[3] = h2_ref[3, pl.ds(JB, R3 * JB), :]
    dn_ref[3] = h2_ref[2, pl.ds(JB, R3 * JB), :]


def weight_grad(x_ref, e_ref, plane, pair, grads, g_ref, first):
    ut = jnp.transpose(grads).astype(bf16)
    for f in range(3):
        rhs = jnp.concatenate(patch(x_ref, e_ref, plane, pair, f, OWN * JB), axis=1)
        part = dotf(ut, rhs, NN)
        g_ref[f] = part if first else g_ref[f] + part


def extract(g_ref, conv, flip, scale, out_ref):
    lanes = lane_block((32, 128))

    def body(f, carry):
        fe = jnp.where(flip == 0, f, 2 - f)
        for e in range(3):
            total = jnp.zeros((32, 128), f32)
            for p in range(2):
                q = p + e
                for jo in range(4):
                    rows = pl.ds(p * 128 + jo * 32, 32)
                    block = g_ref[f, rows, pl.ds(q * 128, 128)]
                    if jo != 1:
                        block = pltpu.roll(block, ((1 - jo) * 32) % 128, 1)
                    if jo == 0:
                        block = jnp.where((lanes == 1) | (lanes == 2), block, 0.0)
                    elif jo == 3:
                        block = jnp.where(lanes < 2, block, 0.0)
                    else:
                        block = jnp.where(lanes < 3, block, 0.0)
                    total = total + block
                    if jo in (0, 3):
                        side = g_ref[f, rows, pl.ds(512 + (q // 2) * 128, 128)]
                        at = 2 * (q % 2)
                        total = total + (one_block(side, at, 0) if jo == 0 else one_block(side, at + 1, 2))
            out_ref[conv * 9 + e * 3 + fe] = total * scale
        return carry

    lax.fori_loop(0, 3, body, 0)


def backward_kernel(
    meta, radii, coords_ref, types_ref, parts_ref, mine_ref, head_ref,
    x_ref, ex_ref, h1_ref, e1_ref, h2_ref, e2_ref, m3_ref, lo_ref, hi_ref, u_ref,
    gw_ref, force_ref, info_ref,
    t_ref, et_ref, mg_ref, em_ref, sg_ref, es_ref, hm_ref, w_ref, acc_ref, g_ref, dg_ref, dk_ref,
    gy_ref, sy_ref, live_ref, y_ref, dy_ref,
):
    flip = meta[1]
    cells = meta[3].astype(f32) * (NXY * NXY)
    head = head_ref[...]
    pooled = jnp.sum(parts_ref[...], axis=0, keepdims=True) / cells
    lane = lax.broadcasted_iota(jnp.int32, (1, 128), 1)
    score = jnp.sum(jnp.where(lane < 32, pooled * head, 0.0), axis=1, keepdims=True)
    sign = (2 * meta[4] - 1).astype(f32)
    score_grad = -sign / (1.0 + jnp.exp(sign * score))
    info_ref[0:1, :] = jnp.broadcast_to(score, (1, 128))
    info_ref[1:2, :] = score_grad * mine_ref[0:1, :] / cells
    info_ref[2:8, :] = jnp.zeros((6, 128), f32)
    tone = rounded(score_grad * head)

    for ref in (t_ref, et_ref, mg_ref, em_ref, sg_ref, es_ref):
        clear_pad(ref)
    mask_of = lambda q: (lo_ref.at[q] if q < 3 else m3_ref.at[q - 3] if q < 7 else hi_ref.at[q - 7])
    for m in range(5):
        for c in range(5):
            sl = pl.ds(c * 112, 112)
            vals = [jnp.where(mask_of(q)[sl, :].astype(f32) > 0.0, tone, 0.0) for q in (2 * m, 2 * m + 1)]
            put_pair(t_ref, et_ref, 2 * m, m, JB + c * 112, *vals)
    hm_ref[0] = lo_ref[3]
    hm_ref[7] = hi_ref[3]
    for k in range(6):
        hm_ref[k + 1] = h2_ref[k, pl.ds(JB, R3 * JB), :]

    scale = 1.0 / cells
    own_rows = pl.ds(JB, OWN * JB)
    for m in range(2):
        grads = jnp.concatenate([t_ref[3 + 2 * m, own_rows, :], t_ref[4 + 2 * m, own_rows, :]], axis=1)
        weight_grad(h2_ref, e2_ref, 2 * m, m, grads, g_ref, m == 0)
    extract(g_ref, 2, flip, scale, gw_ref)

    build_backward(u_ref, 2, flip, w_ref)

    def mid(m, carry):
        conv_pair(t_ref, et_ref, 2 * m, m, RM, w_ref, acc_ref, NN)
        for c in range(NCH):
            sl = pl.ds(c * 112, 112)
            vals = [
                rounded(jnp.where(hm_ref[2 * m + k, sl, :].astype(f32) > 0.0, acc_ref[sl, pl.ds(128 * k, 128)], 0.0))
                for k in range(2)
            ]
            put_pair(mg_ref, em_ref, 2 * m, m, JB + c * 112, *vals)
        return carry

    lax.fori_loop(0, 4, mid, 0)

    for m in range(3):
        ga = mg_ref[1 + 2 * m, own_rows, :]
        gb = mg_ref[2 + 2 * m, own_rows, :]
        if m == 0:
            ga = jnp.zeros_like(ga)
        if m == 2:
            gb = jnp.zeros_like(gb)
        weight_grad(h1_ref, e1_ref, 2 * m, m, jnp.concatenate([ga, gb], axis=1), g_ref, m == 0)
    extract(g_ref, 1, flip, scale, gw_ref)

    build_backward(u_ref, 1, flip, w_ref)

    def low(m, carry):
        conv_pair(mg_ref, em_ref, 2 * m, m, RG, w_ref, acc_ref, NN)
        for c in range(NCH):
            sl = pl.ds(c * 112, 112)
            src = pl.ds(JB + c * 112, 112)
            vals = []
            for k in range(2):
                back = t_ref[2 * m + 2 + k, src, :].astype(f32) + acc_ref[sl, pl.ds(128 * k, 128)]
                vals.append(rounded(jnp.where(h1_ref[2 * m + 1 + k, src, :].astype(f32) > 0.0, back, 0.0)))
            put_pair(sg_ref, es_ref, 2 * m, m, JB + c * 112, *vals)
        return carry

    lax.fori_loop(0, 3, low, 0)

    for m in range(2):
        grads = jnp.concatenate([sg_ref[1 + 2 * m, own_rows, :], sg_ref[2 + 2 * m, own_rows, :]], axis=1)
        weight_grad(x_ref, ex_ref, 2 + 2 * m, 1 + m, grads, g_ref, m == 0)
    extract(g_ref, 0, flip, scale, gw_ref)

    build_backward(u_ref, 0, flip, w_ref)

    def last(m, carry):
        conv_pair(sg_ref, es_ref, 2 * m, m, OWN, w_ref, acc_ref, NN)
        for k in range(2):
            at = pl.ds(pl.multiple_of((2 * m + k) * OWN * JB, 16), OWN * JB)
            dg_ref[at, :] = rounded(acc_ref[pl.ds(0, OWN * JB), pl.ds(128 * k, 128)])
        return carry

    lax.fori_loop(0, 2, last, 0)
    for jb in range(JB):
        dk_ref[:, pl.ds(jb * 128, 128)] = dg_ref[pl.ds(jb, 4 * OWN, stride=JB), :].astype(bf16)

    types = types_ref[...]
    inv_sq = atom_terms(meta, radii, types, 2)
    atoms = types.shape[1]
    gy, off = bump(centre_rows(NXY, 0, 1, 0.5 * NXY), coords_ref[1:2, :], inv_sq)
    gy_ref[...] = gy
    sy_ref[...] = 4.0 * off * inv_sq * gy
    kind = lax.broadcasted_iota(jnp.int32, (32, atoms), 0)
    slot = lax.broadcasted_iota(jnp.int32, (32, atoms), 1)
    live_ref[...] = jnp.where((types == kind) & (slot < meta[2]), 1.0, 0.0)
    top, step = first_row(meta)
    half_z = 0.5 * meta[3].astype(f32)
    wide = 256
    for b in range(atoms // wide):
        sl = pl.ds(b * wide, wide)

        def table(j, carry):
            live = live_ref[:, sl]
            at = pl.ds(pl.multiple_of(j * 32, 32), 32)
            y_ref[at, :] = (live * gy_ref[pl.ds(j, 1), sl]).astype(bf16)
            dy_ref[at, :] = (live * sy_ref[pl.ds(j, 1), sl]).astype(bf16)
            return carry

        lax.fori_loop(0, NXY, table, 0, unroll=4)
        plain = dotf(dk_ref[...], y_ref[...], NN)
        slope = dotf(dk_ref[...], dy_ref[...], NN)
        inv = inv_sq[:, b * wide : (b + 1) * wide]
        gx, off_x = bump(centre_rows(OWN, top, step, 0.5 * NXY), coords_ref[0:1, sl], inv)
        dgx = 4.0 * off_x * inv * gx
        gz, off_z = bump(centre_rows(8, 4 * meta[0], 1, half_z), coords_ref[2:3, sl], inv)
        dgz = 4.0 * off_z * inv * gz
        fx = jnp.zeros((1, wide), f32)
        fy = jnp.zeros((1, wide), f32)
        fz = jnp.zeros((1, wide), f32)
        for k in range(4):
            pk = plain[k * OWN : (k + 1) * OWN, :]
            sk = slope[k * OWN : (k + 1) * OWN, :]
            fx = fx + gz[k : k + 1, :] * jnp.sum(pk * dgx, axis=0, keepdims=True)
            fy = fy + gz[k : k + 1, :] * jnp.sum(sk * gx, axis=0, keepdims=True)
            fz = fz + dgz[k : k + 1, :] * jnp.sum(pk * gx, axis=0, keepdims=True)
        force_ref[0:1, sl] = fx
        force_ref[1:2, sl] = fy
        force_ref[2:3, sl] = fz


def smem():
    return pl.BlockSpec(memory_space=pltpu.SMEM)


def vmem():
    return pl.BlockSpec(memory_space=pltpu.VMEM)


def lane_rows(w):
    o, c = w.shape[:2]
    moved = jnp.transpose(w, (2, 3, 0, 4, 1)).astype(f32)
    moved = jnp.pad(moved, ((0, 0), (0, 0), (0, 0), (0, 1), (0, 32 - c)))
    return moved.reshape(9, o, 128)


def local(coords, atom_types, counts, labels, receptor, radii, w_stem, w_one, w_two, w_head):
    slab_count = lax.axis_size("slab")
    pose_count = lax.axis_size("pose")
    atoms = coords.shape[2]
    s = lax.axis_index("slab")
    group, half = s // 2, s % 2
    depth = receptor.shape[2] * slab_count
    meta = jnp.stack([group, half, counts[0], jnp.int32(depth), labels[0]]).astype(jnp.int32)
    bh = (RD * JB, 128)

    raw = jnp.pad(jnp.transpose(receptor[0], (1, 0, 2)), ((0, 0), (0, 4), (0, 0)))
    mine, theirs = pl.pallas_call(
        pack_kernel,
        out_shape=[jax.ShapeDtypeStruct((2,) + bh, bf16)] * 2,
        in_specs=[smem(), vmem()],
        out_specs=[vmem(), vmem()],
        name="pack",
    )(meta, raw)
    other = lax.ppermute(theirs, "slab", [(i, i ^ 1) for i in range(slab_count)])
    lower = jnp.where(half == 0, mine, other)
    upper = jnp.where(half == 0, other, mine)
    own = jnp.concatenate([lower, upper], axis=0)
    ups = [(i, i + 2) for i in range(slab_count - 2)]
    downs = [(i + 2, i) for i in range(slab_count - 2)]
    lo = lax.ppermute(own[1:4], "slab", ups)
    hi = lax.ppermute(own[0:3], "slab", downs)

    types = atom_types
    splat = pl.pallas_call(
        splat_kernel,
        out_shape=jax.ShapeDtypeStruct((6400, 128), f32),
        in_specs=[smem(), smem(), vmem(), vmem()],
        out_specs=vmem(),
        scratch_shapes=[
            pltpu.VMEM((400, atoms), bf16),
            pltpu.VMEM((NXY, atoms), f32),
            pltpu.VMEM((32, atoms), f32),
            pltpu.VMEM((256, atoms), bf16),
        ],
        cost_estimate=pl.CostEstimate(flops=2 * 400 * 2048 * atoms, bytes_accessed=4_000_000, transcendentals=0),
        name="splat",
    )(meta, radii, coords[0], types)

    u = jnp.concatenate([lane_rows(w_stem), lane_rows(w_one), lane_rows(w_two)], axis=0)

    big = lambda n: jax.ShapeDtypeStruct((n, BR, 128), bf16)
    thin = lambda n: jax.ShapeDtypeStruct((n, R3 * JB, 128), bf16)
    x, ex, h1, e1, h2, e2, m3, up, dn, pool = pl.pallas_call(
        forward_kernel,
        out_shape=[big(10), big(5), big(8), big(4), big(6), big(3), thin(4), thin(4), thin(4),
                   jax.ShapeDtypeStruct((8, 128), f32)],
        in_specs=[smem()] + [vmem()] * 5,
        out_specs=[vmem()] * 10,
        scratch_shapes=[pltpu.VMEM((3, 256, 768), bf16), pltpu.VMEM((BR, 256), f32)],
        name="forward",
    )(meta, splat, lo, own, hi, u)

    from_lo = lax.ppermute(up, "slab", ups)
    from_hi = lax.ppermute(dn, "slab", downs)
    parts = lax.all_to_all(jnp.broadcast_to(pool[:1][None], (slab_count, 1, 128)), "slab", 0, 0)
    parts = parts.reshape(slab_count, 128)
    head = jnp.tile(w_head, 4)[None, :]

    gw, force, info = pl.pallas_call(
        backward_kernel,
        out_shape=[
            jax.ShapeDtypeStruct((27, 32, 128), f32),
            jax.ShapeDtypeStruct((3, atoms), f32),
            jax.ShapeDtypeStruct((8, 128), f32),
        ],
        in_specs=[smem(), smem()] + [vmem()] * 15,
        out_specs=[vmem()] * 3,
        scratch_shapes=[
            pltpu.VMEM((10, BR, 128), bf16), pltpu.VMEM((5, BR, 128), bf16),
            pltpu.VMEM((8, BR, 128), bf16), pltpu.VMEM((4, BR, 128), bf16),
            pltpu.VMEM((6, BR, 128), bf16), pltpu.VMEM((3, BR, 128), bf16),
            pltpu.VMEM((8, R3 * JB, 128), bf16),
            pltpu.VMEM((3, 768, 256), bf16), pltpu.VMEM((BR, 256), f32), pltpu.VMEM((3, 256, 768), f32),
            pltpu.VMEM((4 * OWN * JB, 128), f32), pltpu.VMEM((4 * OWN, 2048), bf16),
            pltpu.VMEM((NXY, atoms), f32), pltpu.VMEM((NXY, atoms), f32), pltpu.VMEM((32, atoms), f32),
            pltpu.VMEM((2048, 256), bf16), pltpu.VMEM((2048, 256), bf16),
        ],
        name="backward",
    )(meta, radii, coords[0], types, parts, pool, head, x, ex, h1, e1, h2, e2, m3, from_lo, from_hi, u)

    count = pose_count * slab_count
    flat = jnp.concatenate([gw.reshape(27 * 32, 128), info[1:2]], axis=0)
    each = -(-flat.shape[0] // count)
    flat = jnp.pad(flat, ((0, each * count - flat.shape[0]), (0, 0))).reshape(pose_count, slab_count, each, 128)
    share = -(-3 * atoms // (slab_count * 128))
    atom_part = jnp.pad(force.reshape(3 * atoms), (0, share * slab_count * 128 - 3 * atoms))
    atom_part = atom_part.reshape(1, slab_count, share, 128)
    same = (lax.axis_index("pose") == jnp.arange(pose_count))[:, None, None, None]
    atom_part = jnp.where(same, atom_part, 0.0)
    message = jnp.concatenate([flat, atom_part], axis=2).reshape(count, each + share, 128)
    got = lax.all_to_all(message, ("pose", "slab"), 0, 0)
    total = jnp.sum(got, axis=0)
    full = lax.all_to_all(jnp.broadcast_to(total[None], (count, each + share, 128)), ("pose", "slab"), 0, 0)
    rows = full[:, :each].reshape(count * each, 128)
    grads = rows[: 27 * 32].reshape(3, 3, 3, 32, 128)[..., :96].reshape(3, 3, 3, 32, 3, 32)
    grads = grads.transpose(0, 3, 5, 1, 2, 4)
    grad_head = rows[27 * 32, :32]
    atom = lax.dynamic_slice_in_dim(
        full.reshape(pose_count, slab_count, each + share, 128), lax.axis_index("pose"), 1, 0
    )[:, :, each:]
    atom_grad = atom.reshape(-1)[: 3 * atoms].reshape(1, 3, atoms)
    scores = info[0, :1]
    label_sign = (2 * labels - 1).astype(f32)
    pose_loss = jax.nn.softplus(-label_sign * scores)
    return scores, pose_loss, atom_grad, grads[0][:, :28], grads[1], grads[2], grad_head


def solution(mesh):
    return jax.shard_map(
        local,
        mesh=mesh,
        in_specs=(
            P("pose", None, None),
            P("pose", None),
            P("pose"),
            P("pose"),
            P("pose", None, "slab", None),
            P(),
            P(),
            P(),
            P(),
            P(),
        ),
        out_specs=(P("pose"), P("pose"), P("pose", None, None), P(), P(), P(), P()),
        check_vma=False,
    )
```

```python
import functools

import jax
import jax.numpy as jnp
from jax import lax
from jax.experimental import pallas as pl
from jax.experimental.pallas import tpu as pltpu
from jax.sharding import PartitionSpec as P


NXY = 64
resolution = 0.375
f32 = jnp.float32
bf16 = jnp.bfloat16

JB = 16
OWN = 32
RD, RS, R2, R3, RM, RG = 38, 37, 36, 35, 34, 33
BR = 41 * JB
CH = 128
NCH = 5
NT = (((1,), (1,)), ((), ()))
NN = (((1,), (0,)), ((), ()))


def dotf(a, b, dims):
    return lax.dot_general(a, b, dims, preferred_element_type=f32)


def lane_block(shape):
    return lax.broadcasted_iota(jnp.int32, shape, 1) // 32


def spread(block, turn):
    if turn == 1:
        return block
    out = pltpu.roll(block, ((turn - 1) * 32) % 128, 1)
    lanes = lane_block(block.shape)
    if turn == 0:
        return jnp.where(lanes == 3, 0.0, out)
    if turn == 3:
        return jnp.where(lanes == 0, 0.0, out)
    return out


def one_block(block, source, target):
    out = pltpu.roll(block, ((target - source) * 32) % 128, 1)
    return jnp.where(lane_block(block.shape) == target, out, 0.0)


def build_forward(u_ref, conv, flip, w_ref):
    zero = jnp.zeros((32, 128), bf16)

    def body(f, carry):
        fe = jnp.where(flip == 0, f, 2 - f)
        us = [u_ref[conv * 9 + e * 3 + fe] for e in range(3)]
        for jo in range(4):
            rows = [pl.ds(p * 128 + jo * 32, 32) for p in range(2)]
            for e in range(3):
                main = spread(us[e], jo).astype(bf16)
                for p in range(2):
                    w_ref[f, rows[p], pl.ds((p + e) * 128, 128)] = main
            w_ref[f, rows[0], pl.ds(3 * 128, 128)] = zero
            w_ref[f, rows[1], pl.ds(0, 128)] = zero
            for p in range(2):
                for half in range(2):
                    edge = zero
                    if jo in (0, 3):
                        parts = []
                        for q in (2 * half, 2 * half + 1):
                            if 0 <= q - p <= 2:
                                at = 2 * (q % 2)
                                parts.append(one_block(us[q - p], 0, at) if jo == 0 else one_block(us[q - p], 2, at + 1))
                        edge = functools.reduce(jnp.add, parts).astype(bf16)
                    w_ref[f, rows[p], pl.ds(512 + half * 128, 128)] = edge
        return carry

    lax.fori_loop(0, 3, body, 0)


def build_backward(u_ref, conv, flip, w_ref):
    zero = jnp.zeros((32, 128), bf16)

    def body(f, carry):
        fe = jnp.where(flip == 0, 2 - f, f)
        for e in range(3):
            u = u_ref[conv * 9 + (2 - e) * 3 + fe]
            tiles = [spread(u, jc).astype(bf16) for jc in range(4)]
            tiles += [one_block(u, 2, 0).astype(bf16), one_block(u, 0, 3).astype(bf16)]
            for p in range(2):
                q = p + e
                lanes = pl.ds(p * 128, 128)
                for jc in range(6):
                    at = q * 128 + jc * 32 if jc < 4 else 512 + q * 64 + (jc - 4) * 32
                    w_ref[f, pl.ds(at, 32), lanes] = tiles[jc]
        for p, q in ((0, 3), (1, 0)):
            lanes = pl.ds(p * 128, 128)
            for jc in range(6):
                at = q * 128 + jc * 32 if jc < 4 else 512 + q * 64 + (jc - 4) * 32
                w_ref[f, pl.ds(at, 32), lanes] = zero
        return carry

    lax.fori_loop(0, 3, body, 0)


def edges(a, b):
    n = a.shape[0]
    lanes = lane_block((n, 128))
    mixed = jnp.where(lanes < 2, pltpu.roll(a, 32, 1), pltpu.roll(b, 96, 1))
    down = pltpu.roll(mixed, 1, 0)
    up = pltpu.roll(mixed, n - 1, 0)
    jb = lax.broadcasted_iota(jnp.int32, (n, 128), 0) % JB
    low = jnp.where(jb == 0, 0.0, down)
    high = jnp.where(jb == JB - 1, 0.0, up)
    return jnp.where(lanes % 2 == 0, low, high)


def patch(x_ref, e_ref, plane, pair, f, n):
    sl = pl.ds(f * JB, n)
    return [x_ref[plane + k, sl, :] for k in range(4)] + [e_ref[pair + k, sl, :] for k in range(2)]


def conv_pair(x_ref, e_ref, plane, pair, rows, w_ref, acc_ref, dims):
    n = rows * JB
    total = None
    for f in range(3):
        lhs = jnp.concatenate(patch(x_ref, e_ref, plane, pair, f, n), axis=1)
        part = dotf(lhs, w_ref[f], dims)
        total = part if total is None else total + part
    acc_ref[pl.ds(0, n), :] = total


def put_pair(main_ref, e_ref, plane, pair, at, va, vb):
    main_ref[plane, pl.ds(at, va.shape[0]), :] = va.astype(bf16)
    main_ref[plane + 1, pl.ds(at, va.shape[0]), :] = vb.astype(bf16)
    if e_ref is not None:
        e_ref[pair, pl.ds(at, va.shape[0]), :] = edges(va, vb).astype(bf16)


def rounded(v):
    return v.astype(bf16).astype(f32)


def clear_pad(ref):
    for k in range(ref.shape[0]):
        ref[k, pl.ds(0, JB), :] = jnp.zeros((JB, 128), ref.dtype)


WIN = 40 * NXY


def pack_planes(h, source, put):
    row = lax.broadcasted_iota(jnp.int32, (256, 256), 0)
    col = lax.broadcasted_iota(jnp.int32, (256, 256), 1)
    mask = jnp.where((row // 32) % 4 == col % 4, 1.0, 0.0).astype(bf16)
    srow = lax.broadcasted_iota(jnp.int32, (64, 256), 0)
    scol = lax.broadcasted_iota(jnp.int32, (64, 256), 1)
    a = srow // JB
    a = jnp.where(h == 0, a, 3 - a)
    pick = jnp.where((srow % JB == (scol // 4) % JB) & (scol // NXY == a), 1.0, 0.0).astype(bf16)
    for ch in range(10):
        at = pl.multiple_of(jnp.where(h == 0, ch, 9 - ch) * 256, 256)
        x0, x1 = source(at)
        wide = jnp.concatenate([x0] * 4 + [x1] * 4, axis=0) * mask
        out = dotf(pick, wide, NT).astype(bf16)
        n = 64 if ch < 9 else 32
        for p in range(2):
            put(p, pl.ds(ch * 64, n), out[:n, p * 128 : (p + 1) * 128])


def widen(raw_ref, wide_ref, sl):
    for p in range(2):
        wide_ref[p, pl.ds(16, 16), :] = jnp.zeros((16, WIN), bf16)
        wide_ref[p, pl.ds(0, raw_ref.shape[1]), :] = raw_ref[p, :, sl]

    def source(at):
        return [wide_ref[p, :, pl.ds(at, 256)] for p in range(2)]

    return source


def pack_own_kernel(raw_ref, out_ref, wide_ref):
    h = place()[1]
    base = pl.multiple_of(jnp.where(h == 0, 0, NXY * NXY - WIN), 256)

    def put(p, sl, val):
        out_ref[p, sl, :] = val

    pack_planes(h, widen(raw_ref, wide_ref, pl.ds(base, WIN)), put)


def pack_kernel(raw_ref, mine_ref, own_ref, up_ref, dn_ref, wide_ref):
    h = place()[1]

    def put(p, sl, val):
        own_ref[2 * (1 - h) + p, sl, :] = val

    pack_planes(h, widen(raw_ref, wide_ref, pl.ds(0, WIN)), put)
    for p in range(2):
        own_ref[2 * h + p] = mine_ref[p]
    for k in range(3):
        up_ref[k] = own_ref[k + 1]
        dn_ref[k] = own_ref[k]


def weights_kernel(u_ref, wf_ref, wb_ref):
    flip = place()[1]
    for conv in range(3):
        build_forward(u_ref, conv, flip, wf_ref.at[conv])
        build_backward(u_ref, conv, flip, wb_ref.at[conv])


def atom_terms(radii, types):
    radius = jnp.zeros(types.shape, f32)
    for c in range(radii.shape[0]):
        radius = radius + jnp.where(types == c, radii[c], 0.0)
    return 1.0 / (radius * radius)


def centre_rows(n, first, step, half):
    row = lax.broadcasted_iota(jnp.int32, (n, 1), 0)
    return ((first + step * row).astype(f32) + 0.5 - half) * resolution


def bump(centre, place, inv_sq):
    offset = centre - place
    return jnp.exp(-2.0 * offset * offset * inv_sq), offset


def first_row(half):
    return jnp.where(half == 0, 0, NXY - 1), jnp.where(half == 0, 1, -1)


def splat_kernel(depth, count, radii, coords_ref, types_ref, out_ref, z_ref, gy_ref, live_ref, y_ref):
    atoms = types_ref.shape[1]
    types = types_ref[...]
    inv_sq = atom_terms(radii, types)
    group, half = place()
    top, step = first_row(half)
    gx = bump(centre_rows(40, top, step, 0.5 * NXY), coords_ref[0], inv_sq)[0]
    gz = bump(centre_rows(16, 4 * group - 3, 1, 0.5 * depth), coords_ref[2], inv_sq)[0]
    for q in range(10):
        z_ref[pl.ds(q * 40, 40), :] = (gz[q : q + 1, :] * gx).astype(bf16)
    gy_ref[...] = bump(centre_rows(NXY, 0, 1, 0.5 * NXY), coords_ref[1], inv_sq)[0]
    kind = lax.broadcasted_iota(jnp.int32, (32, atoms), 0)
    slot = lax.broadcasted_iota(jnp.int32, (32, atoms), 1)
    live_ref[...] = jnp.where((types == kind) & (slot < count[0]), 1.0, 0.0)

    def body(step8, carry):
        for t in range(8):
            y = gy_ref[pl.ds(step8 * 8 + t, 1), :]
            y_ref[pl.ds(t * 32, 32), :] = (live_ref[...] * y).astype(bf16)
        out = dotf(z_ref[...], y_ref[...], NT)
        out_ref[pl.ds(2 * step8, 400, stride=JB), :] = out[:, :128]
        out_ref[pl.ds(2 * step8 + 1, 400, stride=JB), :] = out[:, 128:]
        return carry

    lax.fori_loop(0, 8, body, 0)


def forward_kernel(
    depth, splat_ref, lo_ref, own_ref, hi_ref, w_ref,
    x_ref, ex_ref, h1_ref, e1_ref, h2_ref, e2_ref, m3_ref, up_ref, dn_ref, pool_ref,
    acc_ref,
):
    first = 4 * place()[0] - 3
    for ref in (x_ref, ex_ref, h1_ref, e1_ref, h2_ref, e2_ref):
        clear_pad(ref)

    def inside(q):
        z = first + q
        return jnp.where((z >= 0) & (z < depth), 1.0, 0.0)

    def receptor(q, sl):
        if q < 3:
            return lo_ref[q, sl, :]
        if q < 7:
            return own_ref[q - 3, sl, :]
        return hi_ref[q - 7, sl, :]

    for m in range(5):
        def density(c, carry):
            at = c * 304
            sl = pl.ds(pl.multiple_of(at, 16), 304)
            vals = []
            for q in (2 * m, 2 * m + 1):
                v = splat_ref[pl.ds(pl.multiple_of(q * 640 + at, 16), 304), :] + receptor(q, sl).astype(f32)
                vals.append(rounded(v * inside(q)))
            put_pair(x_ref, ex_ref, 2 * m, m, pl.multiple_of(JB + at, 16), *vals)
            return carry

        lax.fori_loop(0, 2, density, 0)


    def stem(m, carry):
        conv_pair(x_ref, ex_ref, 2 * m, m, RS, w_ref.at[0], acc_ref, NT)
        ia, ib = inside(2 * m + 1), inside(2 * m + 2)
        for c in range(NCH):
            acc = jnp.maximum(acc_ref[pl.ds(c * CH, CH), :], 0.0)
            put_pair(h1_ref, e1_ref, 2 * m, m, JB + c * CH, rounded(acc[:, :128] * ia), rounded(acc[:, 128:] * ib))
        return carry

    lax.fori_loop(0, 4, stem, 0)

    def second(m, carry):
        conv_pair(h1_ref, e1_ref, 2 * m, m, R2, w_ref.at[1], acc_ref, NT)
        ia, ib = inside(2 * m + 2), inside(2 * m + 3)
        for c in range(NCH):
            acc = jnp.maximum(acc_ref[pl.ds(c * CH, CH), :], 0.0)
            put_pair(h2_ref, e2_ref, 2 * m, m, JB + c * CH, rounded(acc[:, :128] * ia), rounded(acc[:, 128:] * ib))
        return carry

    lax.fori_loop(0, 3, second, 0)

    def third(m, pool):
        conv_pair(h2_ref, e2_ref, 2 * m, m, R3, w_ref.at[2], acc_ref, NT)
        for c in range(7):
            sl = pl.ds(c * 80, 80)
            src = pl.ds(JB + c * 80, 80)
            for k in range(2):
                keep = h1_ref[2 * m + 2 + k, src, :].astype(f32)
                summed = keep + acc_ref[sl, pl.ds(128 * k, 128)]
                top = jnp.maximum(summed, 0.0)
                if (c + 1) * 80 > OWN * JB:
                    row = lax.broadcasted_iota(jnp.int32, (80, 128), 0) + c * 80
                    top = jnp.where(row < OWN * JB, top, 0.0)
                pool = pool + jnp.sum(top, axis=0, keepdims=True)
                m3_ref[2 * m + k, sl, :] = jnp.where(summed > 0.0, 1.0, 0.0).astype(bf16)
        return pool

    pool = lax.fori_loop(0, 2, third, jnp.zeros((1, 128), f32))
    pool = pool + pltpu.roll(pool, 64, 1)
    pool = pool + pltpu.roll(pool, 32, 1)
    pool_ref[...] = jnp.broadcast_to(pool, pool_ref.shape)
    for k in range(3):
        up_ref[k] = m3_ref[k + 1]
        dn_ref[k] = m3_ref[k]
    up_ref[3] = h2_ref[3, pl.ds(JB, R3 * JB), :]
    dn_ref[3] = h2_ref[2, pl.ds(JB, R3 * JB), :]


def weight_grad(x_ref, e_ref, plane, pair, grads, g_ref, first):
    ut = jnp.transpose(grads).astype(bf16)
    for f in range(3):
        rhs = jnp.concatenate(patch(x_ref, e_ref, plane, pair, f, OWN * JB), axis=1)
        part = dotf(ut, rhs, NN)
        g_ref[f] = part if first else g_ref[f] + part


def extract(g_ref, flip, scale, put):
    lanes = lane_block((32, 128))

    def body(f, carry):
        fe = jnp.where(flip == 0, f, 2 - f)
        for e in range(3):
            total = jnp.zeros((32, 128), f32)
            for p in range(2):
                q = p + e
                for jo in range(4):
                    rows = pl.ds(p * 128 + jo * 32, 32)
                    block = g_ref[f, rows, pl.ds(q * 128, 128)]
                    if jo != 1:
                        block = pltpu.roll(block, ((1 - jo) * 32) % 128, 1)
                    if jo == 0:
                        block = jnp.where((lanes == 1) | (lanes == 2), block, 0.0)
                    elif jo == 3:
                        block = jnp.where(lanes < 2, block, 0.0)
                    else:
                        block = jnp.where(lanes < 3, block, 0.0)
                    total = total + block
                    if jo in (0, 3):
                        side = g_ref[f, rows, pl.ds(512 + (q // 2) * 128, 128)]
                        at = 2 * (q % 2)
                        total = total + (one_block(side, at, 0) if jo == 0 else one_block(side, at + 1, 2))
            put(e * 3 + fe, total * scale)
        return carry

    lax.fori_loop(0, 3, body, 0)


def prepare_kernel(m3_ref, h2_ref, e2_ref, gw_ref, g_ref):
    flip = place()[1]
    rows = pl.ds(0, OWN * JB)
    for m in range(2):
        grads = jnp.concatenate([m3_ref[2 * m, rows, :], m3_ref[2 * m + 1, rows, :]], axis=1)
        weight_grad(h2_ref, e2_ref, 2 * m, m, grads, g_ref, m == 0)

    def put(k, val):
        gw_ref[k] = val

    extract(g_ref, flip, 1.0, put)


def backward_kernel(
    depth, label, pool_ref, mine_ref, head_ref,
    x_ref, ex_ref, h1_ref, e1_ref, h2_ref, m3_ref, lo_ref, hi_ref, gw2_ref, w_ref,
    keep_ref, give_ref, score_ref, loss_ref, dk_ref,
    t_ref, et_ref, mg_ref, em_ref, sg_ref, es_ref, hm_ref, acc_ref, g_ref, flat_ref, dg_ref,
):
    flip = place()[1]
    scale = 1.0 / (depth * NXY * NXY)
    head = head_ref[...]
    pooled = pool_ref[0:1, :] * scale
    lane = lax.broadcasted_iota(jnp.int32, (1, 128), 1)
    score = jnp.sum(jnp.where(lane < 32, pooled * head, 0.0), axis=1, keepdims=True)
    sign = (2 * label[0] - 1).astype(f32)
    logit = -sign * score
    score_grad = -sign / (1.0 + jnp.exp(-logit))
    loss = jnp.maximum(logit, 0.0) + jnp.log1p(jnp.exp(-jnp.abs(logit)))
    score_ref[0] = jnp.sum(score)
    loss_ref[0] = jnp.sum(loss)
    tone = rounded(score_grad * head)

    half_rows = keep_ref.shape[0]
    lanes = lane_block((32, 128))
    eye = lax.broadcasted_iota(jnp.int32, (32, 128), 0) == lax.broadcasted_iota(jnp.int32, (32, 128), 1)
    tall = jnp.sum(jnp.where(eye, tone, 0.0), axis=1, keepdims=True) * scale
    for k in range(6):
        tile = gw2_ref[k] * tall
        for g in range(3):
            flat_ref[pl.ds((3 * k + g) * 32, 32), :] = one_block(tile, g, 3)
    for k in range(3):
        flat_ref[pl.ds((18 + k) * 32, 32), :] = gw2_ref[6 + k] * tall
    tail = 2 * half_rows - 672
    flat_ref[pl.ds(672, tail), :] = jnp.where(
        lax.broadcasted_iota(jnp.int32, (tail, 128), 0) == 0, score_grad * mine_ref[0:1, :] * scale, 0.0
    )

    def put_rows(conv):
        def put(k, val):
            rows = pl.ds(pl.multiple_of((conv * 9 + k) * 32, 32), 32)
            flat_ref[rows, :] = jnp.where(lanes < 3, val, flat_ref[rows, :])

        return put

    for ref in (t_ref, et_ref, mg_ref, em_ref, sg_ref, es_ref):
        clear_pad(ref)
    mask_of = lambda q: (lo_ref.at[q] if q < 3 else m3_ref.at[q - 3] if q < 7 else hi_ref.at[q - 7])
    for m in range(5):
        for c in range(5):
            sl = pl.ds(c * 112, 112)
            vals = [jnp.where(mask_of(q)[sl, :].astype(f32) > 0.0, tone, 0.0) for q in (2 * m, 2 * m + 1)]
            put_pair(t_ref, et_ref, 2 * m, m, JB + c * 112, *vals)
    hm_ref[0] = lo_ref[3]
    hm_ref[7] = hi_ref[3]
    for k in range(6):
        hm_ref[k + 1] = h2_ref[k, pl.ds(JB, R3 * JB), :]

    own_rows = pl.ds(JB, OWN * JB)

    def mid(m, carry):
        conv_pair(t_ref, et_ref, 2 * m, m, RM, w_ref.at[2], acc_ref, NN)
        for c in range(NCH):
            sl = pl.ds(c * 112, 112)
            vals = [
                rounded(jnp.where(hm_ref[2 * m + k, sl, :].astype(f32) > 0.0, acc_ref[sl, pl.ds(128 * k, 128)], 0.0))
                for k in range(2)
            ]
            put_pair(mg_ref, em_ref, 2 * m, m, JB + c * 112, *vals)
        return carry

    lax.fori_loop(0, 4, mid, 0)

    for m in range(3):
        ga = mg_ref[1 + 2 * m, own_rows, :]
        gb = mg_ref[2 + 2 * m, own_rows, :]
        if m == 0:
            ga = jnp.zeros_like(ga)
        if m == 2:
            gb = jnp.zeros_like(gb)
        weight_grad(h1_ref, e1_ref, 2 * m, m, jnp.concatenate([ga, gb], axis=1), g_ref, m == 0)
    extract(g_ref, flip, scale, put_rows(1))

    def low(m, carry):
        conv_pair(mg_ref, em_ref, 2 * m, m, RG, w_ref.at[1], acc_ref, NN)
        for c in range(NCH):
            sl = pl.ds(c * 112, 112)
            src = pl.ds(JB + c * 112, 112)
            vals = []
            for k in range(2):
                back = t_ref[2 * m + 2 + k, src, :].astype(f32) + acc_ref[sl, pl.ds(128 * k, 128)]
                vals.append(rounded(jnp.where(h1_ref[2 * m + 1 + k, src, :].astype(f32) > 0.0, back, 0.0)))
            put_pair(sg_ref, es_ref, 2 * m, m, JB + c * 112, *vals)
        return carry

    lax.fori_loop(0, 3, low, 0)

    for m in range(2):
        grads = jnp.concatenate([sg_ref[1 + 2 * m, own_rows, :], sg_ref[2 + 2 * m, own_rows, :]], axis=1)
        weight_grad(x_ref, ex_ref, 2 + 2 * m, 1 + m, grads, g_ref, m == 0)
    extract(g_ref, flip, scale, put_rows(0))
    core = lax.axis_index("core")
    keep_ref[...] = flat_ref[pl.ds(pl.multiple_of(core * half_rows, 16), half_rows), :]
    give_ref[...] = flat_ref[pl.ds(pl.multiple_of((1 - core) * half_rows, 16), half_rows), :]

    def last(m, carry):
        conv_pair(sg_ref, es_ref, 2 * m, m, OWN, w_ref.at[0], acc_ref, NN)
        for k in range(2):
            at = pl.ds(pl.multiple_of((2 * m + k) * OWN * JB, 16), OWN * JB)
            dg_ref[at, :] = rounded(acc_ref[pl.ds(0, OWN * JB), pl.ds(128 * k, 128)])
        return carry

    lax.fori_loop(0, 2, last, 0)
    for jb in range(JB):
        dk_ref[:, pl.ds(jb * 128, 128)] = dg_ref[pl.ds(jb, 4 * OWN, stride=JB), :].astype(bf16)


def atom_kernel(depth, count, radii, coords_ref, types_ref, dk_ref, force_ref, gy_ref, sy_ref, live_ref, y_ref, dy_ref):
    types = types_ref[...]
    inv_sq = atom_terms(radii, types)
    atoms = types.shape[1]
    gy, off = bump(centre_rows(NXY, 0, 1, 0.5 * NXY), coords_ref[1], inv_sq)
    gy_ref[...] = gy
    sy_ref[...] = 4.0 * off * inv_sq * gy
    kind = lax.broadcasted_iota(jnp.int32, (32, atoms), 0)
    slot = lax.broadcasted_iota(jnp.int32, (32, atoms), 1)
    live_ref[...] = jnp.where((types == kind) & (slot < count[0]), 1.0, 0.0)
    group, half = place()
    top, step = first_row(half)
    wide = 256
    for b in range(atoms // wide):
        sl = pl.ds(b * wide, wide)

        def table(j, carry):
            live = live_ref[:, sl]
            at = pl.ds(pl.multiple_of(j * 32, 32), 32)
            y_ref[at, :] = (live * gy_ref[pl.ds(j, 1), sl]).astype(bf16)
            dy_ref[at, :] = (live * sy_ref[pl.ds(j, 1), sl]).astype(bf16)
            return carry

        lax.fori_loop(0, NXY, table, 0, unroll=4)
        plain = dotf(dk_ref[...], y_ref[...], NN)
        slope = dotf(dk_ref[...], dy_ref[...], NN)
        inv = inv_sq[:, b * wide : (b + 1) * wide]
        gx, off_x = bump(centre_rows(OWN, top, step, 0.5 * NXY), coords_ref[0, :, sl], inv)
        dgx = 4.0 * off_x * inv * gx
        gz, off_z = bump(centre_rows(8, 4 * group, 1, 0.5 * depth), coords_ref[2, :, sl], inv)
        dgz = 4.0 * off_z * inv * gz
        fx = jnp.zeros((1, wide), f32)
        fy = jnp.zeros((1, wide), f32)
        fz = jnp.zeros((1, wide), f32)
        for k in range(4):
            pk = plain[k * OWN : (k + 1) * OWN, :]
            sk = slope[k * OWN : (k + 1) * OWN, :]
            fx = fx + gz[k : k + 1, :] * jnp.sum(pk * dgx, axis=0, keepdims=True)
            fy = fy + gz[k : k + 1, :] * jnp.sum(sk * gx, axis=0, keepdims=True)
            fz = fz + dgz[k : k + 1, :] * jnp.sum(pk * gx, axis=0, keepdims=True)
        force_ref[0:1, sl] = fx
        force_ref[1:2, sl] = fy
        force_ref[2:3, sl] = fz


def place():
    s = lax.axis_index("slab")
    return s // 2, s % 2


def smem():
    return pl.BlockSpec(memory_space=pltpu.SMEM)


def vmem():
    return pl.BlockSpec(memory_space=pltpu.VMEM)


def lane_rows(w):
    o, c = w.shape[:2]
    moved = jnp.transpose(w, (2, 3, 0, 4, 1)).astype(f32)
    moved = jnp.pad(moved, ((0, 0), (0, 0), (0, 0), (0, 1), (0, 32 - c)))
    return moved.reshape(9, o, 128)


def finish_kernel(mine_ref, other_ref, fa_ref, fb_ref, stem_ref, one_ref, two_ref, head_ref, force_ref, both_ref):
    core = lax.axis_index("core")
    both_ref[core] = mine_ref[...]
    both_ref[1 - core] = other_ref[...]
    half_rows = mine_ref.shape[0]

    def tile(t):
        return both_ref[t * 32 // half_rows, pl.ds(t * 32 % half_rows, 32), :]

    for t in range(27):
        conv, k = divmod(t, 9)
        ref = (stem_ref, one_ref, two_ref)[conv]
        for g in range(3):
            if conv < 2:
                block, at = tile(t), g
            elif k < 6:
                block, at = tile(3 * k + g), 3
            else:
                block, at = tile(12 + k), g
            val = pltpu.roll(block, 128 - 32 * at, 1) if at else block
            ref[3 * k + g] = val[:, : ref.shape[2]]
    head_ref[...] = both_ref[672 // half_rows, pl.ds(672 % half_rows, 8), :][:1, :32]
    total = fa_ref[...] + fb_ref[...]
    for k in range(3):
        force_ref[k] = total[k : k + 1, :]


def call(kernel, limit, flops, **kwargs):
    return pl.pallas_call(
        kernel,
        compiler_params=pltpu.CompilerParams(vmem_limit_bytes=limit << 20),
        cost_estimate=pl.CostEstimate(flops=int(flops), bytes_accessed=4_000_000, transcendentals=0),
        **kwargs,
    )


def local(coords, atom_types, counts, labels, receptor, radii, w_stem, w_one, w_two, w_head):
    slab_count = lax.axis_size("slab")
    y_count = lax.axis_size("y")
    atoms = coords.shape[2]
    half = lax.axis_index("slab") % 2
    depth = receptor.shape[2] * slab_count
    bh = (RD * JB, 128)
    places = coords.reshape(3, 1, atoms)

    raw = jnp.transpose(receptor[0], (1, 0, 2))
    theirs = lax.dynamic_slice_in_dim(raw, jnp.where(half == 1, 0, NXY * NXY - WIN), WIN, 2)
    other = lax.ppermute(theirs, "slab", [(i, i ^ 1) for i in range(slab_count)])
    mine = call(
        pack_own_kernel, 6, 2e9,
        out_shape=jax.ShapeDtypeStruct((2,) + bh, bf16),
        in_specs=[vmem()],
        out_specs=vmem(),
        scratch_shapes=[pltpu.VMEM((2, 32, WIN), bf16)],
    )(raw)
    u = jnp.concatenate([lane_rows(w_stem), lane_rows(w_one), lane_rows(w_two)], axis=0)
    head = jnp.tile(w_head, 4)[None, :]
    wf, wb = call(
        weights_kernel, 6, 3e9,
        out_shape=[jax.ShapeDtypeStruct((3, 3, 256, 768), bf16), jax.ShapeDtypeStruct((3, 3, 768, 256), bf16)],
        in_specs=[vmem()],
        out_specs=[vmem()] * 2,
    )(u)
    other, mine, wf, wb, head = lax.optimization_barrier((other, mine, wf, wb, head))
    own, own_up, own_dn = call(
        pack_kernel, 6, 2e9,
        out_shape=[jax.ShapeDtypeStruct((n,) + bh, bf16) for n in (4, 3, 3)],
        in_specs=[vmem(), vmem()],
        out_specs=[vmem()] * 3,
        scratch_shapes=[pltpu.VMEM((2, 32, WIN), bf16)],
    )(other, mine)
    ups = [(i, i + 2) for i in range(slab_count - 2)]
    downs = [(i + 2, i) for i in range(slab_count - 2)]
    lo = lax.ppermute(own_up, "slab", ups)
    hi = lax.ppermute(own_dn, "slab", downs)

    splat = call(
        functools.partial(splat_kernel, depth), 10, 8e9,
        out_shape=jax.ShapeDtypeStruct((6400, 128), f32),
        in_specs=[smem(), smem(), vmem(), vmem()],
        out_specs=vmem(),
        scratch_shapes=[
            pltpu.VMEM((400, atoms), bf16),
            pltpu.VMEM((NXY, atoms), f32),
            pltpu.VMEM((32, atoms), f32),
            pltpu.VMEM((256, atoms), bf16),
        ],
    )(counts, radii, places, atom_types)

    big = lambda n: jax.ShapeDtypeStruct((n, BR, 128), bf16)
    thin = lambda n: jax.ShapeDtypeStruct((n, R3 * JB, 128), bf16)
    x, ex, h1, e1, h2, e2, m3, up, dn, pool = call(
        functools.partial(forward_kernel, depth), 8, 1.4e10,
        out_shape=[big(10), big(5), big(8), big(4), big(6), big(3), thin(4), thin(4), thin(4),
                   jax.ShapeDtypeStruct((8, 128), f32)],
        in_specs=[vmem()] * 5,
        out_specs=[vmem()] * 10,
        scratch_shapes=[pltpu.VMEM((BR, 256), f32)],
    )(splat, lo, own, hi, wf)

    def over_slab(value, rounds):
        step = 1
        while step < rounds:
            value = value + lax.ppermute(value, "slab", [(i, i ^ step) for i in range(slab_count)])
            step *= 2
        return value

    from_lo = lax.ppermute(up, "slab", ups)
    from_hi = lax.ppermute(dn, "slab", downs)
    pool_sum = over_slab(pool, slab_count)
    gw2 = call(
        prepare_kernel, 8, 3e9,
        out_shape=jax.ShapeDtypeStruct((9, 32, 128), f32),
        in_specs=[vmem()] * 3,
        out_specs=vmem(),
        scratch_shapes=[pltpu.VMEM((3, 256, 768), f32)],
    )(m3, h2, e2)

    ranks = y_count * slab_count
    each = -(-680 // (2 * ranks))
    if each > 8:
        each = -(-each // 8) * 8
    half_rows = each * ranks
    keep, give, scores, pose_loss, dk = call(
        functools.partial(backward_kernel, depth), 18, 1.4e10,
        out_shape=[
            jax.ShapeDtypeStruct((half_rows, 128), f32), jax.ShapeDtypeStruct((half_rows, 128), f32),
            jax.ShapeDtypeStruct((1,), f32), jax.ShapeDtypeStruct((1,), f32),
            jax.ShapeDtypeStruct((4 * OWN, 2048), bf16),
        ],
        in_specs=[smem()] + [vmem()] * 13,
        out_specs=[vmem(), vmem(), smem(), smem(), vmem()],
        scratch_shapes=[
            pltpu.VMEM((10, BR, 128), bf16), pltpu.VMEM((5, BR, 128), bf16),
            pltpu.VMEM((8, BR, 128), bf16), pltpu.VMEM((4, BR, 128), bf16),
            pltpu.VMEM((6, BR, 128), bf16), pltpu.VMEM((3, BR, 128), bf16),
            pltpu.VMEM((8, R3 * JB, 128), bf16),
            pltpu.VMEM((BR, 256), f32), pltpu.VMEM((3, 256, 768), f32),
            pltpu.VMEM((2 * half_rows, 128), f32), pltpu.VMEM((4 * OWN * JB, 128), f32),
        ],
    )(labels, pool_sum, pool, head, x, ex, h1, e1, h2, m3, from_lo, from_hi, gw2, wb)

    swap = [(0, 1), (1, 0)]
    chip = keep + lax.ppermute(give, "core", swap)
    got = lax.all_to_all(chip.reshape(ranks, each, 128), ("y", "slab"), 0, 0)
    force = call(
        functools.partial(atom_kernel, depth), 12, 1e10,
        out_shape=jax.ShapeDtypeStruct((3, atoms), f32),
        in_specs=[smem(), smem(), vmem(), vmem(), vmem()],
        out_specs=vmem(),
        scratch_shapes=[
            pltpu.VMEM((NXY, atoms), f32), pltpu.VMEM((NXY, atoms), f32), pltpu.VMEM((32, atoms), f32),
            pltpu.VMEM((2048, 256), bf16), pltpu.VMEM((2048, 256), bf16),
        ],
    )(counts, radii, places, atom_types, dk)
    total = jnp.sum(got, axis=0)
    total, force = lax.optimization_barrier((total, force))
    spread_total = jnp.broadcast_to(total[None], (ranks, each, 128))
    gathered = lax.all_to_all(spread_total, ("y", "slab"), 0, 0)
    gathered = gathered.reshape(half_rows, 128)
    gathered_other = lax.ppermute(gathered, "core", swap)
    last_step = slab_count // 2
    force = over_slab(force, last_step)
    force_other = lax.ppermute(force, "slab", [(i, i ^ last_step) for i in range(slab_count)])

    grid = lambda c: jax.ShapeDtypeStruct((27, 32, c), f32)
    stem, one, two, grad_head, atom_grad = call(
        finish_kernel, 6, 1e8,
        out_shape=[grid(w_stem.shape[1]), grid(32), grid(32), jax.ShapeDtypeStruct((1, 32), f32),
                   jax.ShapeDtypeStruct((3, 1, atoms), f32)],
        in_specs=[vmem()] * 4,
        out_specs=[vmem()] * 5,
        scratch_shapes=[pltpu.VMEM((2, half_rows, 128), f32)],
    )(gathered, gathered_other, force, force_other)
    shaped = lambda v: v.reshape(3, 3, 3, 32, v.shape[2]).transpose(3, 4, 0, 1, 2)
    return (scores, pose_loss, atom_grad.reshape(1, 3, atoms), shaped(stem), shaped(one), shaped(two),
            grad_head.reshape(32))


def solution(mesh):
    pose_count, slab_count = mesh.shape["pose"], mesh.shape["slab"]
    fine = jax.sharding.Mesh(mesh.devices.reshape(pose_count // 2, 2, slab_count), ("y", "core", "slab"))
    pose = ("y", "core")

    return jax.shard_map(
        local,
        mesh=fine,
        in_specs=(
            P(pose, None, None),
            P(pose, None),
            P(pose),
            P(pose),
            P(pose, None, "slab", None),
            P(),
            P(),
            P(),
            P(),
            P(),
        ),
        out_specs=(P(pose), P(pose), P(pose, None, None), P(), P(), P(), P()),
        check_vma=False,
    )
```

```python
import functools

import jax
import jax.numpy as jnp
from jax import lax
from jax.experimental import pallas as pl
from jax.experimental.pallas import tpu as pltpu
from jax.sharding import PartitionSpec as P


NXY = 64
resolution = 0.375
f32 = jnp.float32
bf16 = jnp.bfloat16

JB = 16
OWN = 32
RD, RS, R2, R3, RM, RG = 38, 37, 36, 35, 34, 33
BR = 41 * JB
CH = 128
NCH = 5
NT = (((1,), (1,)), ((), ()))
NN = (((1,), (0,)), ((), ()))


def dotf(a, b, dims):
    return lax.dot_general(a, b, dims, preferred_element_type=f32)


def lane_block(shape):
    return lax.broadcasted_iota(jnp.int32, shape, 1) // 32


def spread(block, turn):
    if turn == 1:
        return block
    out = pltpu.roll(block, ((turn - 1) * 32) % 128, 1)
    lanes = lane_block(block.shape)
    if turn == 0:
        return jnp.where(lanes == 3, 0.0, out)
    if turn == 3:
        return jnp.where(lanes == 0, 0.0, out)
    return out


def one_block(block, source, target):
    out = pltpu.roll(block, ((target - source) * 32) % 128, 1)
    return jnp.where(lane_block(block.shape) == target, out, 0.0)


def build_forward(u_ref, conv, flip, w_ref):
    zero = jnp.zeros((32, 128), bf16)

    def body(f, carry):
        fe = jnp.where(flip == 0, f, 2 - f)
        at_f = pl.multiple_of(f * 768, 128)
        us = [u_ref[conv * 9 + e * 3 + fe] for e in range(3)]
        for jo in range(4):
            rows = [pl.ds(p * 128 + jo * 32, 32) for p in range(2)]
            for e in range(3):
                main = spread(us[e], jo).astype(bf16)
                for p in range(2):
                    w_ref[rows[p], pl.ds(at_f + (p + e) * 128, 128)] = main
            w_ref[rows[0], pl.ds(at_f + 3 * 128, 128)] = zero
            w_ref[rows[1], pl.ds(at_f, 128)] = zero
            for p in range(2):
                for half in range(2):
                    edge = zero
                    if jo in (0, 3):
                        parts = []
                        for q in (2 * half, 2 * half + 1):
                            if 0 <= q - p <= 2:
                                at = 2 * (q % 2)
                                parts.append(one_block(us[q - p], 0, at) if jo == 0 else one_block(us[q - p], 2, at + 1))
                        edge = functools.reduce(jnp.add, parts).astype(bf16)
                    w_ref[rows[p], pl.ds(at_f + 512 + half * 128, 128)] = edge
        return carry

    lax.fori_loop(0, 3, body, 0)


def build_backward(u_ref, conv, flip, w_ref):
    zero = jnp.zeros((32, 128), bf16)

    def body(f, carry):
        fe = jnp.where(flip == 0, 2 - f, f)
        at_f = pl.multiple_of(f * 768, 128)
        for e in range(3):
            u = u_ref[conv * 9 + (2 - e) * 3 + fe]
            tiles = [spread(u, jc).astype(bf16) for jc in range(4)]
            tiles += [one_block(u, 2, 0).astype(bf16), one_block(u, 0, 3).astype(bf16)]
            for p in range(2):
                q = p + e
                lanes = pl.ds(p * 128, 128)
                for jc in range(6):
                    at = q * 128 + jc * 32 if jc < 4 else 512 + q * 64 + (jc - 4) * 32
                    w_ref[pl.ds(at_f + at, 32), lanes] = tiles[jc]
        for p, q in ((0, 3), (1, 0)):
            lanes = pl.ds(p * 128, 128)
            for jc in range(6):
                at = q * 128 + jc * 32 if jc < 4 else 512 + q * 64 + (jc - 4) * 32
                w_ref[pl.ds(at_f + at, 32), lanes] = zero
        return carry

    lax.fori_loop(0, 3, body, 0)


def edges(a, b):
    n = a.shape[0]
    lanes = lane_block((n, 128))
    mixed = jnp.where(lanes < 2, pltpu.roll(a, 32, 1), pltpu.roll(b, 96, 1))
    down = pltpu.roll(mixed, 1, 0)
    up = pltpu.roll(mixed, n - 1, 0)
    jb = lax.broadcasted_iota(jnp.int32, (n, 128), 0) % JB
    low = jnp.where(jb == 0, 0.0, down)
    high = jnp.where(jb == JB - 1, 0.0, up)
    return jnp.where(lanes % 2 == 0, low, high)


def patch(x_ref, e_ref, plane, pair, f, n):
    sl = pl.ds(f * JB, n)
    return [x_ref[plane + k, sl, :] for k in range(4)] + [e_ref[pair + k, sl, :] for k in range(2)]


def conv_pair(x_ref, e_ref, plane, pair, rows, w_ref, acc_ref, dims):
    n = rows * JB
    lhs = jnp.concatenate([p for f in range(3) for p in patch(x_ref, e_ref, plane, pair, f, n)], axis=1)
    acc_ref[pl.ds(0, n), :] = dotf(lhs, w_ref[...], dims)


def put_pair(main_ref, e_ref, plane, pair, at, va, vb):
    main_ref[plane, pl.ds(at, va.shape[0]), :] = va.astype(bf16)
    main_ref[plane + 1, pl.ds(at, va.shape[0]), :] = vb.astype(bf16)
    if e_ref is not None:
        e_ref[pair, pl.ds(at, va.shape[0]), :] = edges(va, vb).astype(bf16)


def rounded(v):
    return v.astype(bf16).astype(f32)


def clear_pad(ref):
    for k in range(ref.shape[0]):
        ref[k, pl.ds(0, JB), :] = jnp.zeros((JB, 128), ref.dtype)


WIN = 40 * NXY


def pack_planes(h, source, put):
    row = lax.broadcasted_iota(jnp.int32, (256, 256), 0)
    col = lax.broadcasted_iota(jnp.int32, (256, 256), 1)
    mask = jnp.where((row // 32) % 4 == col % 4, 1.0, 0.0).astype(bf16)
    srow = lax.broadcasted_iota(jnp.int32, (64, 256), 0)
    scol = lax.broadcasted_iota(jnp.int32, (64, 256), 1)
    a = srow // JB
    a = jnp.where(h == 0, a, 3 - a)
    pick = jnp.where((srow % JB == (scol // 4) % JB) & (scol // NXY == a), 1.0, 0.0).astype(bf16)
    for ch in range(10):
        at = pl.multiple_of(jnp.where(h == 0, ch, 9 - ch) * 256, 256)
        x0, x1 = source(at)
        wide = jnp.concatenate([x0] * 4 + [x1] * 4, axis=0) * mask
        out = dotf(pick, wide, NT).astype(bf16)
        n = 64 if ch < 9 else 32
        for p in range(2):
            put(p, pl.ds(ch * 64, n), out[:n, p * 128 : (p + 1) * 128])


def widen(raw_ref, wide_ref, sl):
    for p in range(2):
        wide_ref[p, pl.ds(16, 16), :] = jnp.zeros((16, WIN), bf16)
        wide_ref[p, pl.ds(0, raw_ref.shape[1]), :] = raw_ref[p, :, sl]

    def source(at):
        return [wide_ref[p, :, pl.ds(at, 256)] for p in range(2)]

    return source


def pack_own_kernel(raw_ref, low_ref, high_ref, wide_ref):
    h = place()[1]
    base = pl.multiple_of(jnp.where(h == 0, 0, NXY * NXY - WIN), 256)

    def put(p, sl, val):
        (low_ref, high_ref)[p][sl, :] = val

    pack_planes(h, widen(raw_ref, wide_ref, pl.ds(base, WIN)), put)


def pack_kernel(raw_ref, low_ref, high_ref, own_ref, up_ref, dn_ref, wide_ref):
    h = place()[1]

    def put(p, sl, val):
        own_ref[2 * (1 - h) + p, sl, :] = val

    pack_planes(h, widen(raw_ref, wide_ref, pl.ds(0, WIN)), put)
    own_ref[2 * h] = low_ref[...]
    own_ref[2 * h + 1] = high_ref[...]
    for k in range(2):
        up_ref[k] = own_ref[2 - h + k]
        dn_ref[k] = own_ref[1 - h + k]


def weights_kernel(stem_ref, one_ref, two_ref, wf_ref, wb_ref, u_ref):
    flip = place()[1]
    for conv, ref in enumerate((stem_ref, one_ref, two_ref)):
        channels = ref.shape[2]
        blank = jnp.zeros((32, 128 - channels), f32)
        for k in range(9):
            tile = jnp.zeros((32, 128), f32)
            for g in range(3):
                block = jnp.concatenate([ref[3 * k + g].astype(f32), blank], axis=1)
                tile = tile + (pltpu.roll(block, 32 * g, 1) if g else block)
            u_ref[conv * 9 + k] = tile
        build_forward(u_ref, conv, flip, wf_ref.at[conv])
        build_backward(u_ref, conv, flip, wb_ref.at[conv])


def atom_terms(radii, types):
    radius = jnp.zeros(types.shape, f32)
    for c in range(radii.shape[0]):
        radius = radius + jnp.where(types == c, radii[c], 0.0)
    return 1.0 / (radius * radius)


def centre_rows(n, first, step, half):
    row = lax.broadcasted_iota(jnp.int32, (n, 1), 0)
    return ((first + step * row).astype(f32) + 0.5 - half) * resolution


def bump(centre, place, inv_sq):
    offset = centre - place
    return jnp.exp(-2.0 * offset * offset * inv_sq), offset


def first_row(half):
    return jnp.where(half == 0, 0, NXY - 1), jnp.where(half == 0, 1, -1)


def splat_kernel(depth, count, radii, coords_ref, types_ref, out_ref, z_ref, gy_ref, live_ref, y_ref):
    atoms = types_ref.shape[1]
    types = types_ref[...]
    inv_sq = atom_terms(radii, types)
    group, half = place()
    top, step = first_row(half)
    gx = bump(centre_rows(40, top, step, 0.5 * NXY), coords_ref[0], inv_sq)[0]
    gz = bump(centre_rows(16, 4 * group - 3, 1, 0.5 * depth), coords_ref[2], inv_sq)[0]
    for q in range(10):
        z_ref[pl.ds(q * 40, 40), :] = (gz[q : q + 1, :] * gx).astype(bf16)
    gy_ref[...] = bump(centre_rows(NXY, 0, 1, 0.5 * NXY), coords_ref[1], inv_sq)[0]
    kind = lax.broadcasted_iota(jnp.int32, (32, atoms), 0)
    slot = lax.broadcasted_iota(jnp.int32, (32, atoms), 1)
    live_ref[...] = jnp.where((types == kind) & (slot < count[0]), 1.0, 0.0)

    def body(step8, carry):
        for t in range(8):
            y = gy_ref[pl.ds(step8 * 8 + t, 1), :]
            y_ref[pl.ds(t * 32, 32), :] = (live_ref[...] * y).astype(bf16)
        out = dotf(z_ref[...], y_ref[...], NT)
        out_ref[pl.ds(2 * step8, 400, stride=JB), :] = out[:, :128]
        out_ref[pl.ds(2 * step8 + 1, 400, stride=JB), :] = out[:, 128:]
        return carry

    lax.fori_loop(0, 8, body, 0)


def forward_kernel(
    depth, splat_ref, lo_one, lo_two, own_ref, hi_one, hi_two, w_ref,
    x_ref, ex_ref, h1_ref, h2_ref, e2_ref, m3_ref, up_ref, dn_ref, pool_ref,
    accs_ref, rim_ref, e1_ref,
):
    group, half = place()
    first = 4 * group - 3
    for k, (one, two) in enumerate(((lo_one, lo_two), (hi_one, hi_two))):
        rim_ref[k, 2 * half] = one[...]
        rim_ref[k, 1 - half] = two[0]
        rim_ref[k, 2 - half] = two[1]
    for ref in (x_ref, ex_ref, h1_ref, e1_ref, h2_ref, e2_ref):
        clear_pad(ref)

    def inside(q):
        z = first + q
        return jnp.where((z >= 0) & (z < depth), 1.0, 0.0)

    def receptor(q, sl):
        if q < 3:
            return rim_ref[0, q, sl, :]
        if q < 7:
            return own_ref[q - 3, sl, :]
        return rim_ref[1, q - 7, sl, :]

    for m in range(5):
        def density(c, carry):
            at = c * 304
            sl = pl.ds(pl.multiple_of(at, 16), 304)
            vals = []
            for q in (2 * m, 2 * m + 1):
                v = splat_ref[pl.ds(pl.multiple_of(q * 640 + at, 16), 304), :] + receptor(q, sl).astype(f32)
                vals.append(rounded(v * inside(q)))
            put_pair(x_ref, ex_ref, 2 * m, m, pl.multiple_of(JB + at, 16), *vals)
            return carry

        lax.fori_loop(0, 2, density, 0)


    def stem(m, carry):
        acc_ref = accs_ref.at[m % 2]
        conv_pair(x_ref, ex_ref, 2 * m, m, RS, w_ref.at[0], acc_ref, NT)
        ia, ib = inside(2 * m + 1), inside(2 * m + 2)
        for c in range(NCH):
            acc = jnp.maximum(acc_ref[pl.ds(c * CH, CH), :], 0.0)
            put_pair(h1_ref, e1_ref, 2 * m, m, JB + c * CH, rounded(acc[:, :128] * ia), rounded(acc[:, 128:] * ib))
        return carry

    for m in range(4):
        stem(m, 0)

    def second(m, carry):
        acc_ref = accs_ref.at[m % 2]
        conv_pair(h1_ref, e1_ref, 2 * m, m, R2, w_ref.at[1], acc_ref, NT)
        ia, ib = inside(2 * m + 2), inside(2 * m + 3)
        for c in range(NCH):
            acc = jnp.maximum(acc_ref[pl.ds(c * CH, CH), :], 0.0)
            put_pair(h2_ref, e2_ref, 2 * m, m, JB + c * CH, rounded(acc[:, :128] * ia), rounded(acc[:, 128:] * ib))
        return carry

    for m in range(3):
        second(m, 0)

    def third(m, pool):
        acc_ref = accs_ref.at[m % 2]
        conv_pair(h2_ref, e2_ref, 2 * m, m, R3, w_ref.at[2], acc_ref, NT)
        for c in range(7):
            sl = pl.ds(c * 80, 80)
            src = pl.ds(JB + c * 80, 80)
            for k in range(2):
                keep = h1_ref[2 * m + 2 + k, src, :].astype(f32)
                summed = keep + acc_ref[sl, pl.ds(128 * k, 128)]
                top = jnp.maximum(summed, 0.0)
                if (c + 1) * 80 > OWN * JB:
                    row = lax.broadcasted_iota(jnp.int32, (80, 128), 0) + c * 80
                    top = jnp.where(row < OWN * JB, top, 0.0)
                pool = pool + jnp.sum(top, axis=0, keepdims=True)
                m3_ref[2 * m + k, sl, :] = jnp.where(summed > 0.0, 1.0, 0.0).astype(bf16)
        return pool

    pool = jnp.zeros((1, 128), f32)
    for m in range(2):
        pool = third(m, pool)
    pool = pool + pltpu.roll(pool, 64, 1)
    pool = pool + pltpu.roll(pool, 32, 1)
    pool_ref[...] = jnp.broadcast_to(pool, pool_ref.shape)
    for k in range(3):
        up_ref[k] = m3_ref[k + 1]
        dn_ref[k] = m3_ref[k]
    up_ref[3] = h2_ref[3, pl.ds(JB, R3 * JB), :]
    dn_ref[3] = h2_ref[2, pl.ds(JB, R3 * JB), :]


def weight_grad(x_ref, e_ref, plane, pair, grads, g_ref, first):
    ut = jnp.transpose(grads).astype(bf16)
    for f in range(3):
        rhs = jnp.concatenate(patch(x_ref, e_ref, plane, pair, f, OWN * JB), axis=1)
        part = dotf(ut, rhs, NN)
        g_ref[f] = part if first else g_ref[f] + part


def extract(g_ref, flip, scale, put):
    lanes = lane_block((32, 128))

    def body(f, carry):
        fe = jnp.where(flip == 0, f, 2 - f)
        for e in range(3):
            total = jnp.zeros((32, 128), f32)
            for p in range(2):
                q = p + e
                for jo in range(4):
                    rows = pl.ds(p * 128 + jo * 32, 32)
                    block = g_ref[f, rows, pl.ds(q * 128, 128)]
                    if jo != 1:
                        block = pltpu.roll(block, ((1 - jo) * 32) % 128, 1)
                    if jo == 0:
                        block = jnp.where((lanes == 1) | (lanes == 2), block, 0.0)
                    elif jo == 3:
                        block = jnp.where(lanes < 2, block, 0.0)
                    else:
                        block = jnp.where(lanes < 3, block, 0.0)
                    total = total + block
                    if jo in (0, 3):
                        side = g_ref[f, rows, pl.ds(512 + (q // 2) * 128, 128)]
                        at = 2 * (q % 2)
                        total = total + (one_block(side, at, 0) if jo == 0 else one_block(side, at + 1, 2))
            put(e * 3 + fe, total * scale)
        return carry

    lax.fori_loop(0, 3, body, 0)


def prepare_kernel(m3_ref, h2_ref, e2_ref, h1_ref, gw_ref, e1_ref, g_ref):
    flip = place()[1]
    clear_pad(e1_ref)
    for m in range(3):
        for c in range(5):
            sl = pl.ds(JB + c * CH, CH)
            sides = [h1_ref[2 * m + 1 + k, sl, :].astype(f32) for k in range(2)]
            e1_ref[m, sl, :] = edges(*sides).astype(bf16)
    rows = pl.ds(0, OWN * JB)
    for m in range(2):
        grads = jnp.concatenate([m3_ref[2 * m, rows, :], m3_ref[2 * m + 1, rows, :]], axis=1)
        weight_grad(h2_ref, e2_ref, 2 * m, m, grads, g_ref, m == 0)

    def put(k, val):
        gw_ref[k] = val

    extract(g_ref, flip, 1.0, put)


def backward_kernel(
    depth, terms, label, *refs,
):
    pool_refs, refs = refs[:terms], refs[terms:]
    mine_ref, head_ref, x_ref, ex_ref, h1_ref, e1_ref, h2_ref, m3_ref, lo_ref, hi_ref, gw2_ref, w_ref = refs[:12]
    keep_ref, give_ref, score_ref, loss_ref, dk_ref = refs[12:17]
    t_ref, et_ref, mg_ref, em_ref, sg_ref, es_ref, hm_ref, accs_ref, g_ref, flat_ref, dg_ref = refs[17:]
    flip = place()[1]
    scale = 1.0 / (depth * NXY * NXY)
    head = head_ref[...]
    pooled = terms_sum([ref[0:1, :] for ref in pool_refs]) * scale
    lane = lax.broadcasted_iota(jnp.int32, (1, 128), 1)
    score = jnp.sum(jnp.where(lane < 32, pooled * head, 0.0), axis=1, keepdims=True)
    sign = (2 * label[0] - 1).astype(f32)
    logit = -sign * score
    score_grad = -sign / (1.0 + jnp.exp(-logit))
    loss = jnp.maximum(logit, 0.0) + jnp.log1p(jnp.exp(-jnp.abs(logit)))
    score_ref[0] = jnp.sum(score)
    loss_ref[0] = jnp.sum(loss)
    tone = rounded(score_grad * head)

    half_rows = keep_ref.shape[0]
    lanes = lane_block((32, 128))
    eye = lax.broadcasted_iota(jnp.int32, (32, 128), 0) == lax.broadcasted_iota(jnp.int32, (32, 128), 1)
    tall = jnp.sum(jnp.where(eye, tone, 0.0), axis=1, keepdims=True) * scale
    for k in range(6):
        tile = gw2_ref[k] * tall
        for g in range(3):
            flat_ref[pl.ds((3 * k + g) * 32, 32), :] = one_block(tile, g, 3)
    for k in range(3):
        flat_ref[pl.ds((18 + k) * 32, 32), :] = gw2_ref[6 + k] * tall
    tail = 2 * half_rows - 672
    flat_ref[pl.ds(672, tail), :] = jnp.where(
        lax.broadcasted_iota(jnp.int32, (tail, 128), 0) == 0, score_grad * mine_ref[0:1, :] * scale, 0.0
    )

    def put_rows(conv):
        def put(k, val):
            rows = pl.ds(pl.multiple_of((conv * 9 + k) * 32, 32), 32)
            flat_ref[rows, :] = jnp.where(lanes < 3, val, flat_ref[rows, :])

        return put

    for ref in (t_ref, et_ref, mg_ref, em_ref, sg_ref, es_ref):
        clear_pad(ref)
    mask_of = lambda q: (lo_ref.at[q] if q < 3 else m3_ref.at[q - 3] if q < 7 else hi_ref.at[q - 7])
    for m in range(5):
        for c in range(5):
            sl = pl.ds(c * 112, 112)
            vals = [jnp.where(mask_of(q)[sl, :].astype(f32) > 0.0, tone, 0.0) for q in (2 * m, 2 * m + 1)]
            put_pair(t_ref, et_ref, 2 * m, m, JB + c * 112, *vals)
    hm_ref[0] = lo_ref[3]
    hm_ref[7] = hi_ref[3]
    for k in range(6):
        hm_ref[k + 1] = h2_ref[k, pl.ds(JB, R3 * JB), :]

    own_rows = pl.ds(JB, OWN * JB)

    def mid(m, carry):
        acc_ref = accs_ref.at[m % 2]
        conv_pair(t_ref, et_ref, 2 * m, m, RM, w_ref.at[2], acc_ref, NN)
        for c in range(NCH):
            sl = pl.ds(c * 112, 112)
            vals = [
                rounded(jnp.where(hm_ref[2 * m + k, sl, :].astype(f32) > 0.0, acc_ref[sl, pl.ds(128 * k, 128)], 0.0))
                for k in range(2)
            ]
            put_pair(mg_ref, em_ref, 2 * m, m, JB + c * 112, *vals)
        return carry

    for m in range(4):
        mid(m, 0)

    for m in range(2):
        grads = jnp.concatenate([mg_ref[2 + 2 * m, own_rows, :], mg_ref[3 + 2 * m, own_rows, :]], axis=1)
        weight_grad(h1_ref, e1_ref, 1 + 2 * m, m, grads, g_ref, m == 0)
    extract(g_ref, flip, scale, put_rows(1))

    def low(m, carry):
        acc_ref = accs_ref.at[m % 2]
        conv_pair(mg_ref, em_ref, 2 * m, m, RG, w_ref.at[1], acc_ref, NN)
        for c in range(NCH):
            sl = pl.ds(c * 112, 112)
            src = pl.ds(JB + c * 112, 112)
            vals = []
            for k in range(2):
                back = t_ref[2 * m + 2 + k, src, :].astype(f32) + acc_ref[sl, pl.ds(128 * k, 128)]
                vals.append(rounded(jnp.where(h1_ref[2 * m + 1 + k, src, :].astype(f32) > 0.0, back, 0.0)))
            put_pair(sg_ref, es_ref, 2 * m, m, JB + c * 112, *vals)
        return carry

    for m in range(3):
        low(m, 0)

    for m in range(2):
        grads = jnp.concatenate([sg_ref[1 + 2 * m, own_rows, :], sg_ref[2 + 2 * m, own_rows, :]], axis=1)
        weight_grad(x_ref, ex_ref, 2 + 2 * m, 1 + m, grads, g_ref, m == 0)
    extract(g_ref, flip, scale, put_rows(0))
    core = lax.axis_index("core")
    keep_ref[...] = flat_ref[pl.ds(pl.multiple_of(core * half_rows, 16), half_rows), :]
    give_ref[...] = flat_ref[pl.ds(pl.multiple_of((1 - core) * half_rows, 16), half_rows), :]

    def last(m, carry):
        acc_ref = accs_ref.at[m % 2]
        conv_pair(sg_ref, es_ref, 2 * m, m, OWN, w_ref.at[0], acc_ref, NN)
        for k in range(2):
            at = pl.ds(pl.multiple_of((2 * m + k) * OWN * JB, 16), OWN * JB)
            dg_ref[at, :] = rounded(acc_ref[pl.ds(0, OWN * JB), pl.ds(128 * k, 128)])
        return carry

    for m in range(2):
        last(m, 0)
    for jb in range(JB):
        dk_ref[:, pl.ds(jb * 128, 128)] = dg_ref[pl.ds(jb, 4 * OWN, stride=JB), :].astype(bf16)


def atom_kernel(depth, count, radii, coords_ref, types_ref, dk_ref, force_ref, gy_ref, sy_ref, live_ref, y_ref, dy_ref):
    types = types_ref[...]
    inv_sq = atom_terms(radii, types)
    atoms = types.shape[1]
    gy, off = bump(centre_rows(NXY, 0, 1, 0.5 * NXY), coords_ref[1], inv_sq)
    gy_ref[...] = gy
    sy_ref[...] = 4.0 * off * inv_sq * gy
    kind = lax.broadcasted_iota(jnp.int32, (32, atoms), 0)
    slot = lax.broadcasted_iota(jnp.int32, (32, atoms), 1)
    live_ref[...] = jnp.where((types == kind) & (slot < count[0]), 1.0, 0.0)
    group, half = place()
    top, step = first_row(half)
    wide = 256
    for b in range(atoms // wide):
        sl = pl.ds(b * wide, wide)

        def table(j, carry):
            live = live_ref[:, sl]
            at = pl.ds(pl.multiple_of(j * 32, 32), 32)
            y_ref[at, :] = (live * gy_ref[pl.ds(j, 1), sl]).astype(bf16)
            dy_ref[at, :] = (live * sy_ref[pl.ds(j, 1), sl]).astype(bf16)
            return carry

        lax.fori_loop(0, NXY, table, 0, unroll=4)
        plain = dotf(dk_ref[...], y_ref[...], NN)
        slope = dotf(dk_ref[...], dy_ref[...], NN)
        inv = inv_sq[:, b * wide : (b + 1) * wide]
        gx, off_x = bump(centre_rows(OWN, top, step, 0.5 * NXY), coords_ref[0, :, sl], inv)
        dgx = 4.0 * off_x * inv * gx
        gz, off_z = bump(centre_rows(8, 4 * group, 1, 0.5 * depth), coords_ref[2, :, sl], inv)
        dgz = 4.0 * off_z * inv * gz
        fx = jnp.zeros((1, wide), f32)
        fy = jnp.zeros((1, wide), f32)
        fz = jnp.zeros((1, wide), f32)
        for k in range(4):
            pk = plain[k * OWN : (k + 1) * OWN, :]
            sk = slope[k * OWN : (k + 1) * OWN, :]
            fx = fx + gz[k : k + 1, :] * jnp.sum(pk * dgx, axis=0, keepdims=True)
            fy = fy + gz[k : k + 1, :] * jnp.sum(sk * gx, axis=0, keepdims=True)
            fz = fz + dgz[k : k + 1, :] * jnp.sum(pk * gx, axis=0, keepdims=True)
        force_ref[0:1, sl] = fx
        force_ref[1:2, sl] = fy
        force_ref[2:3, sl] = fz


def terms_sum(terms):
    if len(terms) == 1:
        return terms[0]
    half = len(terms) // 2
    return terms_sum([a + b for a, b in zip(terms[:half], terms[half:])])


def place():
    s = lax.axis_index("slab")
    return s // 2, s % 2


def smem():
    return pl.BlockSpec(memory_space=pltpu.SMEM)


def vmem():
    return pl.BlockSpec(memory_space=pltpu.VMEM)


def finish_kernel(mine_ref, other_ref, sum_ref, stem_ref, one_ref, two_ref, head_ref, force_ref, both_ref):
    core = lax.axis_index("core")
    both_ref[core] = mine_ref[...]
    both_ref[1 - core] = other_ref[...]
    half_rows = mine_ref.shape[0]

    def tile(t):
        return both_ref[t * 32 // half_rows, pl.ds(t * 32 % half_rows, 32), :]

    for t in range(27):
        conv, k = divmod(t, 9)
        ref = (stem_ref, one_ref, two_ref)[conv]
        for g in range(3):
            if conv < 2:
                block, at = tile(t), g
            elif k < 6:
                block, at = tile(3 * k + g), 3
            else:
                block, at = tile(12 + k), g
            val = pltpu.roll(block, 128 - 32 * at, 1) if at else block
            ref[3 * k + g] = val[:, : ref.shape[2]]
    head_ref[...] = both_ref[672 // half_rows, pl.ds(672 % half_rows, 8), :][:1, :32]
    for k in range(3):
        force_ref[k] = sum_ref[k : k + 1, :]


def call(kernel, limit, flops, **kwargs):
    return pl.pallas_call(
        kernel,
        compiler_params=pltpu.CompilerParams(vmem_limit_bytes=limit << 20),
        cost_estimate=pl.CostEstimate(flops=int(flops), bytes_accessed=4_000_000, transcendentals=0),
        **kwargs,
    )


def local(coords, atom_types, counts, labels, receptor, radii, w_stem, w_one, w_two, w_head):
    slab_count = lax.axis_size("slab")
    y_count = lax.axis_size("y")
    atoms = coords.shape[2]
    half = lax.axis_index("slab") % 2
    depth = receptor.shape[2] * slab_count
    bh = (RD * JB, 128)
    places = coords.reshape(3, 1, atoms)

    raw = jnp.transpose(receptor[0], (1, 0, 2))
    theirs = lax.dynamic_slice_in_dim(raw, jnp.where(half == 1, 0, NXY * NXY - WIN), WIN, 2)
    other = lax.ppermute(theirs, "slab", [(i, i ^ 1) for i in range(slab_count)])
    low, high = call(
        pack_own_kernel, 6, 2e9,
        out_shape=[jax.ShapeDtypeStruct(bh, bf16)] * 2,
        in_specs=[vmem()],
        out_specs=[vmem()] * 2,
        scratch_shapes=[pltpu.VMEM((2, 32, WIN), bf16)],
    )(raw)
    offsets = lambda w: jnp.transpose(w, (2, 3, 4, 0, 1)).reshape(27, 32, w.shape[1])
    head = jnp.tile(w_head, 4)[None, :]
    ups = [(i, i + 2) for i in range(slab_count - 2)]
    downs = [(i + 2, i) for i in range(slab_count - 2)]
    lo_one = lax.ppermute(high, "slab", ups)
    hi_one = lax.ppermute(low, "slab", downs)
    wf, wb = call(
        weights_kernel, 6, 3e9,
        out_shape=[jax.ShapeDtypeStruct((3, 256, 2304), bf16), jax.ShapeDtypeStruct((3, 2304, 256), bf16)],
        in_specs=[vmem()] * 3,
        out_specs=[vmem()] * 2,
        scratch_shapes=[pltpu.VMEM((27, 32, 128), f32)],
    )(offsets(w_stem), offsets(w_one), offsets(w_two))
    other, wf, wb, head = lax.optimization_barrier((other, wf, wb, head))
    own, own_up, own_dn = call(
        pack_kernel, 6, 2e9,
        out_shape=[jax.ShapeDtypeStruct((n,) + bh, bf16) for n in (4, 2, 2)],
        in_specs=[vmem()] * 3,
        out_specs=[vmem()] * 3,
        scratch_shapes=[pltpu.VMEM((2, 32, WIN), bf16)],
    )(other, low, high)
    lo_two = lax.ppermute(own_up, "slab", ups)
    hi_two = lax.ppermute(own_dn, "slab", downs)

    splat = call(
        functools.partial(splat_kernel, depth), 10, 8e9,
        out_shape=jax.ShapeDtypeStruct((6400, 128), f32),
        in_specs=[smem(), smem(), vmem(), vmem()],
        out_specs=vmem(),
        scratch_shapes=[
            pltpu.VMEM((400, atoms), bf16),
            pltpu.VMEM((NXY, atoms), f32),
            pltpu.VMEM((32, atoms), f32),
            pltpu.VMEM((256, atoms), bf16),
        ],
    )(counts, radii, places, atom_types)

    big = lambda n: jax.ShapeDtypeStruct((n, BR, 128), bf16)
    thin = lambda n: jax.ShapeDtypeStruct((n, R3 * JB, 128), bf16)
    x, ex, h1, h2, e2, m3, up, dn, pool = call(
        functools.partial(forward_kernel, depth), 8, 1.4e10,
        out_shape=[big(10), big(5), big(8), big(6), big(3), thin(4), thin(4), thin(4),
                   jax.ShapeDtypeStruct((8, 128), f32)],
        in_specs=[vmem()] * 7,
        out_specs=[vmem()] * 9,
        scratch_shapes=[
            pltpu.VMEM((2, BR, 256), f32), pltpu.VMEM((2, 3) + bh, bf16), pltpu.VMEM((4, BR, 128), bf16),
        ],
    )(splat, lo_one, lo_two, own, hi_one, hi_two, wf)

    def swapped(value, bits):
        return lax.ppermute(value, "slab", [(i, i ^ bits) for i in range(slab_count)])

    def slab_terms(value):
        other = swapped(value, 1)
        value = value + other
        bits = 2
        while slab_count // bits > 4:
            value = value + swapped(value, bits)
            bits *= 2
        return [value] + [swapped(value, k) for k in range(bits, slab_count, bits)]

    from_lo = lax.ppermute(up, "slab", ups)
    from_hi = lax.ppermute(dn, "slab", downs)
    pools = slab_terms(pool)
    gw2, e1 = call(
        prepare_kernel, 8, 3e9,
        out_shape=[jax.ShapeDtypeStruct((9, 32, 128), f32), big(3)],
        in_specs=[vmem()] * 4,
        out_specs=[vmem()] * 2,
        scratch_shapes=[pltpu.VMEM((3, 256, 768), f32)],
    )(m3, h2, e2, h1)

    ranks = y_count * slab_count
    each = -(-680 // (2 * ranks))
    if each > 8:
        each = -(-each // 8) * 8
    half_rows = each * ranks
    keep, give, scores, pose_loss, dk = call(
        functools.partial(backward_kernel, depth, len(pools)), 18, 1.4e10,
        out_shape=[
            jax.ShapeDtypeStruct((half_rows, 128), f32), jax.ShapeDtypeStruct((half_rows, 128), f32),
            jax.ShapeDtypeStruct((1,), f32), jax.ShapeDtypeStruct((1,), f32),
            jax.ShapeDtypeStruct((4 * OWN, 2048), bf16),
        ],
        in_specs=[smem()] + [vmem()] * (12 + len(pools)),
        out_specs=[vmem(), vmem(), smem(), smem(), vmem()],
        scratch_shapes=[
            pltpu.VMEM((10, BR, 128), bf16), pltpu.VMEM((5, BR, 128), bf16),
            pltpu.VMEM((8, BR, 128), bf16), pltpu.VMEM((4, BR, 128), bf16),
            pltpu.VMEM((6, BR, 128), bf16), pltpu.VMEM((3, BR, 128), bf16),
            pltpu.VMEM((8, R3 * JB, 128), bf16),
            pltpu.VMEM((2, BR, 256), f32), pltpu.VMEM((3, 256, 768), f32),
            pltpu.VMEM((2 * half_rows, 128), f32), pltpu.VMEM((4 * OWN * JB, 128), f32),
        ],
    )(labels, *pools, pool, head, x, ex, h1, e1, h2, m3, from_lo, from_hi, gw2, wb)

    swap = [(0, 1), (1, 0)]
    chip = keep + lax.ppermute(give, "core", swap)
    got = lax.all_to_all(chip.reshape(ranks, each, 128), ("y", "slab"), 0, 0)
    force = call(
        functools.partial(atom_kernel, depth), 12, 1e10,
        out_shape=jax.ShapeDtypeStruct((3, atoms), f32),
        in_specs=[smem(), smem(), vmem(), vmem(), vmem()],
        out_specs=vmem(),
        scratch_shapes=[
            pltpu.VMEM((NXY, atoms), f32), pltpu.VMEM((NXY, atoms), f32), pltpu.VMEM((32, atoms), f32),
            pltpu.VMEM((2048, 256), bf16), pltpu.VMEM((2048, 256), bf16),
        ],
    )(counts, radii, places, atom_types, dk)
    total = jnp.sum(got, axis=0)
    total, force = lax.optimization_barrier((total, force))
    spread_total = jnp.broadcast_to(total[None], (ranks, each, 128))
    gathered = lax.all_to_all(spread_total, ("y", "slab"), 0, 0)
    gathered = gathered.reshape(half_rows, 128)
    gathered_other = lax.ppermute(gathered, "core", swap)
    forces = slab_terms(force)
    force = terms_sum(forces)

    grid = lambda c: jax.ShapeDtypeStruct((27, 32, c), f32)
    stem, one, two, grad_head, atom_grad = call(
        finish_kernel, 6, 1e8,
        out_shape=[grid(w_stem.shape[1]), grid(32), grid(32), jax.ShapeDtypeStruct((1, 32), f32),
                   jax.ShapeDtypeStruct((3, 1, atoms), f32)],
        in_specs=[vmem()] * 3,
        out_specs=[vmem()] * 5,
        scratch_shapes=[pltpu.VMEM((2, half_rows, 128), f32)],
    )(gathered, gathered_other, force)
    shaped = lambda v: v.reshape(3, 3, 3, 32, v.shape[2]).transpose(3, 4, 0, 1, 2)
    return (scores, pose_loss, atom_grad.reshape(1, 3, atoms), shaped(stem), shaped(one), shaped(two),
            grad_head.reshape(32))


def solution(mesh):
    pose_count, slab_count = mesh.shape["pose"], mesh.shape["slab"]
    fine = jax.sharding.Mesh(mesh.devices.reshape(pose_count // 2, 2, slab_count), ("y", "core", "slab"))
    pose = ("y", "core")

    return jax.shard_map(
        local,
        mesh=fine,
        in_specs=(
            P(pose, None, None),
            P(pose, None),
            P(pose),
            P(pose),
            P(pose, None, "slab", None),
            P(),
            P(),
            P(),
            P(),
            P(),
        ),
        out_specs=(P(pose), P(pose), P(pose, None, None), P(), P(), P(), P()),
        check_vma=False,
    )
```

```python
import functools

import jax
import jax.numpy as jnp
from jax import lax
from jax.experimental import pallas as pl
from jax.experimental.pallas import tpu as pltpu
from jax.sharding import PartitionSpec as P


NXY = 64
resolution = 0.375
f32 = jnp.float32
bf16 = jnp.bfloat16

JB = 16
OWN = 32
RD, RS, R2, R3, RM, RG = 38, 37, 36, 35, 34, 33
BR = 41 * JB
CH = 128
NCH = 5
NT = (((1,), (1,)), ((), ()))
NN = (((1,), (0,)), ((), ()))


def dotf(a, b, dims):
    return lax.dot_general(a, b, dims, preferred_element_type=f32)


def lane_block(shape):
    return lax.broadcasted_iota(jnp.int32, shape, 1) // 32


def spread(block, turn):
    if turn == 1:
        return block
    out = pltpu.roll(block, ((turn - 1) * 32) % 128, 1)
    lanes = lane_block(block.shape)
    if turn == 0:
        return jnp.where(lanes == 3, 0.0, out)
    if turn == 3:
        return jnp.where(lanes == 0, 0.0, out)
    return out


def one_block(block, source, target):
    out = pltpu.roll(block, ((target - source) * 32) % 128, 1)
    return jnp.where(lane_block(block.shape) == target, out, 0.0)


def build_forward(u_ref, conv, flip, w_ref):
    zero = jnp.zeros((32, 128), bf16)

    def body(f, carry):
        fe = jnp.where(flip == 0, f, 2 - f)
        at_f = pl.multiple_of(f * 768, 128)
        us = [u_ref[conv * 9 + e * 3 + fe] for e in range(3)]
        for jo in range(4):
            rows = [pl.ds(p * 128 + jo * 32, 32) for p in range(2)]
            for e in range(3):
                main = spread(us[e], jo).astype(bf16)
                for p in range(2):
                    w_ref[rows[p], pl.ds(at_f + (p + e) * 128, 128)] = main
            w_ref[rows[0], pl.ds(at_f + 3 * 128, 128)] = zero
            w_ref[rows[1], pl.ds(at_f, 128)] = zero
            for p in range(2):
                for half in range(2):
                    edge = zero
                    if jo in (0, 3):
                        parts = []
                        for q in (2 * half, 2 * half + 1):
                            if 0 <= q - p <= 2:
                                at = 2 * (q % 2)
                                parts.append(one_block(us[q - p], 0, at) if jo == 0 else one_block(us[q - p], 2, at + 1))
                        edge = functools.reduce(jnp.add, parts).astype(bf16)
                    w_ref[rows[p], pl.ds(at_f + 512 + half * 128, 128)] = edge
        return carry

    lax.fori_loop(0, 3, body, 0)


def build_backward(u_ref, conv, flip, w_ref):
    zero = jnp.zeros((32, 128), bf16)

    def body(f, carry):
        fe = jnp.where(flip == 0, 2 - f, f)
        at_f = pl.multiple_of(f * 768, 128)
        for e in range(3):
            u = u_ref[conv * 9 + (2 - e) * 3 + fe]
            tiles = [spread(u, jc).astype(bf16) for jc in range(4)]
            tiles += [one_block(u, 2, 0).astype(bf16), one_block(u, 0, 3).astype(bf16)]
            for p in range(2):
                q = p + e
                lanes = pl.ds(p * 128, 128)
                for jc in range(6):
                    at = q * 128 + jc * 32 if jc < 4 else 512 + q * 64 + (jc - 4) * 32
                    w_ref[pl.ds(at_f + at, 32), lanes] = tiles[jc]
        for p, q in ((0, 3), (1, 0)):
            lanes = pl.ds(p * 128, 128)
            for jc in range(6):
                at = q * 128 + jc * 32 if jc < 4 else 512 + q * 64 + (jc - 4) * 32
                w_ref[pl.ds(at_f + at, 32), lanes] = zero
        return carry

    lax.fori_loop(0, 3, body, 0)


def edges(a, b):
    n = a.shape[0]
    lanes = lane_block((n, 128))
    mixed = jnp.where(lanes < 2, pltpu.roll(a, 32, 1), pltpu.roll(b, 96, 1))
    down = pltpu.roll(mixed, 1, 0)
    up = pltpu.roll(mixed, n - 1, 0)
    jb = lax.broadcasted_iota(jnp.int32, (n, 128), 0) % JB
    low = jnp.where(jb == 0, 0.0, down)
    high = jnp.where(jb == JB - 1, 0.0, up)
    return jnp.where(lanes % 2 == 0, low, high)


def patch(x_ref, e_ref, plane, pair, f, n):
    sl = pl.ds(f * JB, n)
    return [x_ref[plane + k, sl, :] for k in range(4)] + [e_ref[pair + k, sl, :] for k in range(2)]


def conv_pair(x_ref, e_ref, plane, pair, rows, w_ref, acc_ref, dims):
    n = rows * JB
    lhs = jnp.concatenate([p for f in range(3) for p in patch(x_ref, e_ref, plane, pair, f, n)], axis=1)
    acc_ref[pl.ds(0, n), :] = dotf(lhs, w_ref[...], dims)


def put_pair(main_ref, e_ref, plane, pair, at, va, vb):
    main_ref[plane, pl.ds(at, va.shape[0]), :] = va.astype(bf16)
    main_ref[plane + 1, pl.ds(at, va.shape[0]), :] = vb.astype(bf16)
    if e_ref is not None:
        e_ref[pair, pl.ds(at, va.shape[0]), :] = edges(va, vb).astype(bf16)


def rounded(v):
    return v.astype(bf16).astype(f32)


def clear_pad(ref):
    for k in range(ref.shape[0]):
        ref[k, pl.ds(0, JB), :] = jnp.zeros((JB, 128), ref.dtype)


WIN = 40 * NXY


def pack_planes(h, source, put):
    row = lax.broadcasted_iota(jnp.int32, (256, 256), 0)
    col = lax.broadcasted_iota(jnp.int32, (256, 256), 1)
    mask = jnp.where((row // 32) % 4 == col % 4, 1.0, 0.0).astype(bf16)
    srow = lax.broadcasted_iota(jnp.int32, (64, 256), 0)
    scol = lax.broadcasted_iota(jnp.int32, (64, 256), 1)
    a = srow // JB
    a = jnp.where(h == 0, a, 3 - a)
    pick = jnp.where((srow % JB == (scol // 4) % JB) & (scol // NXY == a), 1.0, 0.0).astype(bf16)
    for ch in range(10):
        at = pl.multiple_of(jnp.where(h == 0, ch, 9 - ch) * 256, 256)
        x0, x1 = source(at)
        wide = jnp.concatenate([x0] * 4 + [x1] * 4, axis=0) * mask
        out = dotf(pick, wide, NT).astype(bf16)
        n = 64 if ch < 9 else 32
        for p in range(2):
            put(p, pl.ds(ch * 64, n), out[:n, p * 128 : (p + 1) * 128])


def widen(raw_ref, wide_ref, sl):
    for p in range(2):
        wide_ref[p, pl.ds(16, 16), :] = jnp.zeros((16, WIN), bf16)
        wide_ref[p, pl.ds(0, raw_ref.shape[1]), :] = raw_ref[p, :, sl]

    def source(at):
        return [wide_ref[p, :, pl.ds(at, 256)] for p in range(2)]

    return source


def pack_own_kernel(raw_ref, low_ref, high_ref, wide_ref):
    h = place()[1]
    base = pl.multiple_of(jnp.where(h == 0, 0, NXY * NXY - WIN), 256)

    def put(p, sl, val):
        (low_ref, high_ref)[p][sl, :] = val

    pack_planes(h, widen(raw_ref, wide_ref, pl.ds(base, WIN)), put)


def pack_kernel(raw_ref, low_ref, high_ref, own_ref, up_ref, dn_ref, wide_ref):
    h = place()[1]

    def put(p, sl, val):
        own_ref[2 * (1 - h) + p, sl, :] = val

    pack_planes(h, widen(raw_ref, wide_ref, pl.ds(0, WIN)), put)
    own_ref[2 * h] = low_ref[...]
    own_ref[2 * h + 1] = high_ref[...]
    for k in range(2):
        up_ref[k] = own_ref[2 - h + k]
        dn_ref[k] = own_ref[1 - h + k]


def weights_kernel(stem_ref, one_ref, two_ref, wf_ref, u_ref):
    flip = place()[1]
    for conv, ref in enumerate((stem_ref, one_ref, two_ref)):
        channels = ref.shape[2]
        blank = jnp.zeros((32, 128 - channels), f32)
        for k in range(9):
            tile = jnp.zeros((32, 128), f32)
            for g in range(3):
                block = jnp.concatenate([ref[3 * k + g].astype(f32), blank], axis=1)
                tile = tile + (pltpu.roll(block, 32 * g, 1) if g else block)
            u_ref[conv * 9 + k] = tile
        build_forward(u_ref, conv, flip, wf_ref.at[conv])


def atom_terms(radii, types):
    radius = jnp.zeros(types.shape, f32)
    for c in range(radii.shape[0]):
        radius = radius + jnp.where(types == c, radii[c], 0.0)
    return 1.0 / (radius * radius)


def centre_rows(n, first, step, half):
    row = lax.broadcasted_iota(jnp.int32, (n, 1), 0)
    return ((first + step * row).astype(f32) + 0.5 - half) * resolution


def bump(centre, place, inv_sq):
    offset = centre - place
    return jnp.exp(-2.0 * offset * offset * inv_sq), offset


def first_row(half):
    return jnp.where(half == 0, 0, NXY - 1), jnp.where(half == 0, 1, -1)


def splat_kernel(depth, count, radii, coords_ref, types_ref, out_ref, z_ref, gy_ref, live_ref, y_ref):
    atoms = types_ref.shape[1]
    types = types_ref[...]
    inv_sq = atom_terms(radii, types)
    group, half = place()
    top, step = first_row(half)
    gx = bump(centre_rows(40, top, step, 0.5 * NXY), coords_ref[0], inv_sq)[0]
    gz = bump(centre_rows(16, 4 * group - 3, 1, 0.5 * depth), coords_ref[2], inv_sq)[0]
    for q in range(10):
        z_ref[pl.ds(q * 40, 40), :] = (gz[q : q + 1, :] * gx).astype(bf16)
    gy_ref[...] = bump(centre_rows(NXY, 0, 1, 0.5 * NXY), coords_ref[1], inv_sq)[0]
    kind = lax.broadcasted_iota(jnp.int32, (32, atoms), 0)
    slot = lax.broadcasted_iota(jnp.int32, (32, atoms), 1)
    live_ref[...] = jnp.where((types == kind) & (slot < count[0]), 1.0, 0.0)

    def body(step8, carry):
        for t in range(8):
            y = gy_ref[pl.ds(step8 * 8 + t, 1), :]
            y_ref[pl.ds(t * 32, 32), :] = (live_ref[...] * y).astype(bf16)
        out = dotf(z_ref[...], y_ref[...], NT)
        out_ref[pl.ds(2 * step8, 400, stride=JB), :] = out[:, :128]
        out_ref[pl.ds(2 * step8 + 1, 400, stride=JB), :] = out[:, 128:]
        return carry

    lax.fori_loop(0, 8, body, 0)


def forward_kernel(
    depth, splat_ref, lo_one, lo_two, own_ref, hi_one, hi_two, w_ref,
    x_ref, ex_ref, h1_ref, h2_ref, e2_ref, m3_ref, up_ref, dn_ref, pool_ref,
    accs_ref, rim_ref, e1_ref,
):
    group, half = place()
    first = 4 * group - 3
    for k, (one, two) in enumerate(((lo_one, lo_two), (hi_one, hi_two))):
        rim_ref[k, 2 * half] = one[...]
        rim_ref[k, 1 - half] = two[0]
        rim_ref[k, 2 - half] = two[1]
    for ref in (x_ref, ex_ref, h1_ref, e1_ref, h2_ref, e2_ref):
        clear_pad(ref)

    def inside(q):
        z = first + q
        return jnp.where((z >= 0) & (z < depth), 1.0, 0.0)

    def kept(acc, q):
        parts = acc[:, :128], acc[:, 128:]
        return [v if 3 <= q + k < 7 else v * inside(q + k) for k, v in enumerate(parts)]

    def receptor(q, sl):
        if q < 3:
            return rim_ref[0, q, sl, :]
        if q < 7:
            return own_ref[q - 3, sl, :]
        return rim_ref[1, q - 7, sl, :]

    for m in range(5):
        def density(c, carry):
            at = c * 304
            sl = pl.ds(pl.multiple_of(at, 16), 304)
            vals = []
            for q in (2 * m, 2 * m + 1):
                v = splat_ref[pl.ds(pl.multiple_of(q * 640 + at, 16), 304), :] + receptor(q, sl).astype(f32)
                vals.append(v if 3 <= q < 7 else v * inside(q))
            put_pair(x_ref, ex_ref, 2 * m, m, pl.multiple_of(JB + at, 16), *vals)
            return carry

        lax.fori_loop(0, 2, density, 0)


    def stem(m, carry):
        acc_ref = accs_ref.at[m % 2]
        conv_pair(x_ref, ex_ref, 2 * m, m, RS, w_ref.at[0], acc_ref, NT)
        for c in range(NCH):
            acc = jnp.maximum(acc_ref[pl.ds(c * CH, CH), :], 0.0)
            put_pair(h1_ref, e1_ref, 2 * m, m, JB + c * CH, *kept(acc, 2 * m + 1))
        return carry

    for m in range(4):
        stem(m, 0)

    def second(m, carry):
        acc_ref = accs_ref.at[m % 2]
        conv_pair(h1_ref, e1_ref, 2 * m, m, R2, w_ref.at[1], acc_ref, NT)
        for c in range(NCH):
            acc = jnp.maximum(acc_ref[pl.ds(c * CH, CH), :], 0.0)
            put_pair(h2_ref, e2_ref, 2 * m, m, JB + c * CH, *kept(acc, 2 * m + 2))
        return carry

    for m in range(3):
        second(m, 0)

    def third(m, pool):
        acc_ref = accs_ref.at[m % 2]
        conv_pair(h2_ref, e2_ref, 2 * m, m, R3, w_ref.at[2], acc_ref, NT)
        for c in range(7):
            sl = pl.ds(c * 80, 80)
            src = pl.ds(JB + c * 80, 80)
            for k in range(2):
                keep = h1_ref[2 * m + 2 + k, src, :].astype(f32)
                summed = keep + acc_ref[sl, pl.ds(128 * k, 128)]
                top = jnp.maximum(summed, 0.0)
                if (c + 1) * 80 > OWN * JB:
                    row = lax.broadcasted_iota(jnp.int32, (80, 128), 0) + c * 80
                    top = jnp.where(row < OWN * JB, top, 0.0)
                pool = pool + jnp.sum(top, axis=0, keepdims=True)
                m3_ref[2 * m + k, sl, :] = jnp.where(summed > 0.0, 1.0, 0.0).astype(bf16)
        return pool

    pool = jnp.zeros((1, 128), f32)
    for m in range(2):
        pool = third(m, pool)
    pool = pool + pltpu.roll(pool, 64, 1)
    pool = pool + pltpu.roll(pool, 32, 1)
    pool_ref[...] = jnp.broadcast_to(pool, pool_ref.shape)
    for k in range(3):
        up_ref[k] = m3_ref[k + 1]
        dn_ref[k] = m3_ref[k]
    up_ref[3] = h2_ref[3, pl.ds(JB, R3 * JB), :]
    dn_ref[3] = h2_ref[2, pl.ds(JB, R3 * JB), :]


def weight_grad(x_ref, e_ref, plane, pair, grads, g_ref, first):
    ut = jnp.transpose(grads).astype(bf16)
    for f in range(3):
        rhs = jnp.concatenate(patch(x_ref, e_ref, plane, pair, f, OWN * JB), axis=1)
        part = dotf(ut, rhs, NN)
        g_ref[f] = part if first else g_ref[f] + part


def extract(g_ref, flip, scale, put):
    lanes = lane_block((32, 128))

    def body(f, carry):
        fe = jnp.where(flip == 0, f, 2 - f)
        for e in range(3):
            total = jnp.zeros((32, 128), f32)
            for p in range(2):
                q = p + e
                for jo in range(4):
                    rows = pl.ds(p * 128 + jo * 32, 32)
                    block = g_ref[f, rows, pl.ds(q * 128, 128)]
                    if jo != 1:
                        block = pltpu.roll(block, ((1 - jo) * 32) % 128, 1)
                    if jo == 0:
                        block = jnp.where((lanes == 1) | (lanes == 2), block, 0.0)
                    elif jo == 3:
                        block = jnp.where(lanes < 2, block, 0.0)
                    else:
                        block = jnp.where(lanes < 3, block, 0.0)
                    total = total + block
                    if jo in (0, 3):
                        side = g_ref[f, rows, pl.ds(512 + (q // 2) * 128, 128)]
                        at = 2 * (q % 2)
                        total = total + (one_block(side, at, 0) if jo == 0 else one_block(side, at + 1, 2))
            put(e * 3 + fe, total * scale)
        return carry

    lax.fori_loop(0, 3, body, 0)


def prepare_kernel(m3_ref, h2_ref, e2_ref, h1_ref, u_ref, gw_ref, e1_ref, wb_ref, g_ref):
    flip = place()[1]
    for conv in range(3):
        build_backward(u_ref, conv, flip, wb_ref.at[conv])
    clear_pad(e1_ref)
    for m in range(3):
        for c in range(5):
            sl = pl.ds(JB + c * CH, CH)
            sides = [h1_ref[2 * m + 1 + k, sl, :].astype(f32) for k in range(2)]
            e1_ref[m, sl, :] = edges(*sides).astype(bf16)
    rows = pl.ds(0, OWN * JB)
    for m in range(2):
        grads = jnp.concatenate([m3_ref[2 * m, rows, :], m3_ref[2 * m + 1, rows, :]], axis=1)
        weight_grad(h2_ref, e2_ref, 2 * m, m, grads, g_ref, m == 0)

    def put(k, val):
        gw_ref[k] = val

    extract(g_ref, flip, 1.0, put)


def backward_kernel(
    depth, terms, label, *refs,
):
    pool_refs, refs = refs[:terms], refs[terms:]
    mine_ref, head_ref, x_ref, ex_ref, h1_ref, e1_ref, h2_ref, m3_ref, lo_ref, hi_ref, gw2_ref, w_ref = refs[:12]
    keep_ref, give_ref, score_ref, loss_ref, dk_ref = refs[12:17]
    t_ref, et_ref, mg_ref, em_ref, sg_ref, es_ref, hm_ref, accs_ref, g_ref, flat_ref, dg_ref = refs[17:]
    flip = place()[1]
    scale = 1.0 / (depth * NXY * NXY)
    head = head_ref[...]
    pooled = terms_sum([ref[0:1, :] for ref in pool_refs]) * scale
    lane = lax.broadcasted_iota(jnp.int32, (1, 128), 1)
    score = jnp.sum(jnp.where(lane < 32, pooled * head, 0.0), axis=1, keepdims=True)
    sign = (2 * label[0] - 1).astype(f32)
    logit = -sign * score
    score_grad = -sign / (1.0 + jnp.exp(-logit))
    loss = jnp.maximum(logit, 0.0) + jnp.log1p(jnp.exp(-jnp.abs(logit)))
    score_ref[0] = jnp.sum(score)
    loss_ref[0] = jnp.sum(loss)
    tone = rounded(score_grad * head)

    half_rows = keep_ref.shape[0]
    lanes = lane_block((32, 128))
    eye = lax.broadcasted_iota(jnp.int32, (32, 128), 0) == lax.broadcasted_iota(jnp.int32, (32, 128), 1)
    tall = jnp.sum(jnp.where(eye, tone, 0.0), axis=1, keepdims=True) * scale
    for k in range(6):
        tile = gw2_ref[k] * tall
        for g in range(3):
            flat_ref[pl.ds((3 * k + g) * 32, 32), :] = one_block(tile, g, 3)
    for k in range(3):
        flat_ref[pl.ds((18 + k) * 32, 32), :] = gw2_ref[6 + k] * tall
    tail = 2 * half_rows - 672
    flat_ref[pl.ds(672, tail), :] = jnp.where(
        lax.broadcasted_iota(jnp.int32, (tail, 128), 0) == 0, score_grad * mine_ref[0:1, :] * scale, 0.0
    )

    def put_rows(conv):
        def put(k, val):
            rows = pl.ds(pl.multiple_of((conv * 9 + k) * 32, 32), 32)
            flat_ref[rows, :] = jnp.where(lanes < 3, val, flat_ref[rows, :])

        return put

    for ref in (t_ref, et_ref, mg_ref, em_ref, sg_ref, es_ref):
        clear_pad(ref)
    mask_of = lambda q: (lo_ref.at[q] if q < 3 else m3_ref.at[q - 3] if q < 7 else hi_ref.at[q - 7])
    for m in range(5):
        for c in range(5):
            sl = pl.ds(c * 112, 112)
            vals = [jnp.where(mask_of(q)[sl, :].astype(f32) > 0.0, tone, 0.0) for q in (2 * m, 2 * m + 1)]
            put_pair(t_ref, et_ref, 2 * m, m, JB + c * 112, *vals)
    hm_ref[0] = lo_ref[3]
    hm_ref[7] = hi_ref[3]
    for k in range(6):
        hm_ref[k + 1] = h2_ref[k, pl.ds(JB, R3 * JB), :]

    own_rows = pl.ds(JB, OWN * JB)

    def mid(m, carry):
        acc_ref = accs_ref.at[m % 2]
        conv_pair(t_ref, et_ref, 2 * m, m, RM, w_ref.at[2], acc_ref, NN)
        for c in range(NCH):
            sl = pl.ds(c * 112, 112)
            vals = [
                jnp.where(hm_ref[2 * m + k, sl, :].astype(f32) > 0.0, acc_ref[sl, pl.ds(128 * k, 128)], 0.0)
                for k in range(2)
            ]
            put_pair(mg_ref, em_ref, 2 * m, m, JB + c * 112, *vals)
        return carry

    for m in range(4):
        mid(m, 0)

    for m in range(2):
        grads = jnp.concatenate([mg_ref[2 + 2 * m, own_rows, :], mg_ref[3 + 2 * m, own_rows, :]], axis=1)
        weight_grad(h1_ref, e1_ref, 1 + 2 * m, m, grads, g_ref, m == 0)
    extract(g_ref, flip, scale, put_rows(1))

    def low(m, carry):
        acc_ref = accs_ref.at[m % 2]
        conv_pair(mg_ref, em_ref, 2 * m, m, RG, w_ref.at[1], acc_ref, NN)
        for c in range(NCH):
            sl = pl.ds(c * 112, 112)
            src = pl.ds(JB + c * 112, 112)
            vals = []
            for k in range(2):
                back = t_ref[2 * m + 2 + k, src, :].astype(f32) + acc_ref[sl, pl.ds(128 * k, 128)]
                vals.append(jnp.where(h1_ref[2 * m + 1 + k, src, :].astype(f32) > 0.0, back, 0.0))
            put_pair(sg_ref, es_ref, 2 * m, m, JB + c * 112, *vals)
        return carry

    for m in range(3):
        low(m, 0)

    for m in range(2):
        grads = jnp.concatenate([sg_ref[1 + 2 * m, own_rows, :], sg_ref[2 + 2 * m, own_rows, :]], axis=1)
        weight_grad(x_ref, ex_ref, 2 + 2 * m, 1 + m, grads, g_ref, m == 0)
    extract(g_ref, flip, scale, put_rows(0))
    core = lax.axis_index("core")
    keep_ref[...] = flat_ref[pl.ds(pl.multiple_of(core * half_rows, 16), half_rows), :]
    give_ref[...] = flat_ref[pl.ds(pl.multiple_of((1 - core) * half_rows, 16), half_rows), :]

    def last(m, carry):
        acc_ref = accs_ref.at[m % 2]
        conv_pair(sg_ref, es_ref, 2 * m, m, OWN, w_ref.at[0], acc_ref, NN)
        for k in range(2):
            at = pl.ds(pl.multiple_of((2 * m + k) * OWN * JB, 16), OWN * JB)
            dg_ref[at, :] = acc_ref[pl.ds(0, OWN * JB), pl.ds(128 * k, 128)]
        return carry

    for m in range(2):
        last(m, 0)
    for jb in range(JB):
        dk_ref[:, pl.ds(jb * 128, 128)] = dg_ref[pl.ds(jb, 4 * OWN, stride=JB), :].astype(bf16)


def atom_kernel(depth, count, radii, coords_ref, types_ref, dk_ref, force_ref, gy_ref, sy_ref, live_ref, y_ref, dy_ref):
    types = types_ref[...]
    inv_sq = atom_terms(radii, types)
    atoms = types.shape[1]
    gy, off = bump(centre_rows(NXY, 0, 1, 0.5 * NXY), coords_ref[1], inv_sq)
    gy_ref[...] = gy
    sy_ref[...] = 4.0 * off * inv_sq * gy
    kind = lax.broadcasted_iota(jnp.int32, (32, atoms), 0)
    slot = lax.broadcasted_iota(jnp.int32, (32, atoms), 1)
    live_ref[...] = jnp.where((types == kind) & (slot < count[0]), 1.0, 0.0)
    group, half = place()
    top, step = first_row(half)
    wide = 256
    for b in range(atoms // wide):
        sl = pl.ds(b * wide, wide)

        def table(j, carry):
            live = live_ref[:, sl]
            at = pl.ds(pl.multiple_of(j * 32, 32), 32)
            y_ref[at, :] = (live * gy_ref[pl.ds(j, 1), sl]).astype(bf16)
            dy_ref[at, :] = (live * sy_ref[pl.ds(j, 1), sl]).astype(bf16)
            return carry

        lax.fori_loop(0, NXY, table, 0, unroll=4)
        plain = dotf(dk_ref[...], y_ref[...], NN)
        slope = dotf(dk_ref[...], dy_ref[...], NN)
        inv = inv_sq[:, b * wide : (b + 1) * wide]
        gx, off_x = bump(centre_rows(OWN, top, step, 0.5 * NXY), coords_ref[0, :, sl], inv)
        dgx = 4.0 * off_x * inv * gx
        gz, off_z = bump(centre_rows(8, 4 * group, 1, 0.5 * depth), coords_ref[2, :, sl], inv)
        dgz = 4.0 * off_z * inv * gz
        fx = jnp.zeros((1, wide), f32)
        fy = jnp.zeros((1, wide), f32)
        fz = jnp.zeros((1, wide), f32)
        for k in range(4):
            pk = plain[k * OWN : (k + 1) * OWN, :]
            sk = slope[k * OWN : (k + 1) * OWN, :]
            fx = fx + gz[k : k + 1, :] * jnp.sum(pk * dgx, axis=0, keepdims=True)
            fy = fy + gz[k : k + 1, :] * jnp.sum(sk * gx, axis=0, keepdims=True)
            fz = fz + dgz[k : k + 1, :] * jnp.sum(pk * gx, axis=0, keepdims=True)
        force_ref[0:1, sl] = fx
        force_ref[1:2, sl] = fy
        force_ref[2:3, sl] = fz


def terms_sum(terms):
    if len(terms) == 1:
        return terms[0]
    half = len(terms) // 2
    return terms_sum([a + b for a, b in zip(terms[:half], terms[half:])])


def place():
    s = lax.axis_index("slab")
    return s // 2, s % 2


def smem():
    return pl.BlockSpec(memory_space=pltpu.SMEM)


def vmem():
    return pl.BlockSpec(memory_space=pltpu.VMEM)


def finish_kernel(mine_ref, other_ref, sum_ref, stem_ref, one_ref, two_ref, head_ref, force_ref, both_ref):
    core = lax.axis_index("core")
    both_ref[core] = mine_ref[...]
    both_ref[1 - core] = other_ref[...]
    half_rows = mine_ref.shape[0]

    def tile(t):
        return both_ref[t * 32 // half_rows, pl.ds(t * 32 % half_rows, 32), :]

    for t in range(27):
        conv, k = divmod(t, 9)
        ref = (stem_ref, one_ref, two_ref)[conv]
        for g in range(3):
            if conv < 2:
                block, at = tile(t), g
            elif k < 6:
                block, at = tile(3 * k + g), 3
            else:
                block, at = tile(12 + k), g
            val = pltpu.roll(block, 128 - 32 * at, 1) if at else block
            ref[3 * k + g] = val[:, : ref.shape[2]]
    head_ref[...] = both_ref[672 // half_rows, pl.ds(672 % half_rows, 8), :][:1, :32]
    for k in range(3):
        force_ref[k] = sum_ref[k : k + 1, :]


def call(kernel, limit, flops, **kwargs):
    return pl.pallas_call(
        kernel,
        compiler_params=pltpu.CompilerParams(vmem_limit_bytes=limit << 20),
        cost_estimate=pl.CostEstimate(flops=int(flops), bytes_accessed=4_000_000, transcendentals=0),
        **kwargs,
    )


def local(coords, atom_types, counts, labels, receptor, radii, w_stem, w_one, w_two, w_head):
    slab_count = lax.axis_size("slab")
    y_count = lax.axis_size("y")
    atoms = coords.shape[2]
    half = lax.axis_index("slab") % 2
    depth = receptor.shape[2] * slab_count
    bh = (RD * JB, 128)
    places = coords.reshape(3, 1, atoms)

    raw = jnp.transpose(receptor[0], (1, 0, 2))
    theirs = lax.dynamic_slice_in_dim(raw, jnp.where(half == 1, 0, NXY * NXY - WIN), WIN, 2)
    other = lax.ppermute(theirs, "slab", [(i, i ^ 1) for i in range(slab_count)])
    low, high = call(
        pack_own_kernel, 6, 2e9,
        out_shape=[jax.ShapeDtypeStruct(bh, bf16)] * 2,
        in_specs=[vmem()],
        out_specs=[vmem()] * 2,
        scratch_shapes=[pltpu.VMEM((2, 32, WIN), bf16)],
    )(raw)
    offsets = lambda w: jnp.transpose(w, (2, 3, 4, 0, 1)).reshape(27, 32, w.shape[1])
    head = jnp.tile(w_head, 4)[None, :]
    ups = [(i, i + 2) for i in range(slab_count - 2)]
    downs = [(i + 2, i) for i in range(slab_count - 2)]
    lo_one = lax.ppermute(high, "slab", ups)
    hi_one = lax.ppermute(low, "slab", downs)
    other, head = lax.optimization_barrier((other, head))
    own, own_up, own_dn = call(
        pack_kernel, 6, 2e9,
        out_shape=[jax.ShapeDtypeStruct((n,) + bh, bf16) for n in (4, 2, 2)],
        in_specs=[vmem()] * 3,
        out_specs=[vmem()] * 3,
        scratch_shapes=[pltpu.VMEM((2, 32, WIN), bf16)],
    )(other, low, high)
    lo_two = lax.ppermute(own_up, "slab", ups)
    hi_two = lax.ppermute(own_dn, "slab", downs)

    own, w_stem, w_one, w_two = lax.optimization_barrier((own, w_stem, w_one, w_two))
    wf, u = call(
        weights_kernel, 6, 3e9,
        out_shape=[jax.ShapeDtypeStruct((3, 256, 2304), bf16), jax.ShapeDtypeStruct((27, 32, 128), f32)],
        in_specs=[vmem()] * 3,
        out_specs=[vmem()] * 2,
    )(offsets(w_stem), offsets(w_one), offsets(w_two))
    splat = call(
        functools.partial(splat_kernel, depth), 10, 8e9,
        out_shape=jax.ShapeDtypeStruct((6400, 128), f32),
        in_specs=[smem(), smem(), vmem(), vmem()],
        out_specs=vmem(),
        scratch_shapes=[
            pltpu.VMEM((400, atoms), bf16),
            pltpu.VMEM((NXY, atoms), f32),
            pltpu.VMEM((32, atoms), f32),
            pltpu.VMEM((256, atoms), bf16),
        ],
    )(counts, radii, places, atom_types)

    big = lambda n: jax.ShapeDtypeStruct((n, BR, 128), bf16)
    thin = lambda n: jax.ShapeDtypeStruct((n, R3 * JB, 128), bf16)
    x, ex, h1, h2, e2, m3, up, dn, pool = call(
        functools.partial(forward_kernel, depth), 8, 1.4e10,
        out_shape=[big(10), big(5), big(8), big(6), big(3), thin(4), thin(4), thin(4),
                   jax.ShapeDtypeStruct((8, 128), f32)],
        in_specs=[vmem()] * 7,
        out_specs=[vmem()] * 9,
        scratch_shapes=[
            pltpu.VMEM((2, BR, 256), f32), pltpu.VMEM((2, 3) + bh, bf16), pltpu.VMEM((4, BR, 128), bf16),
        ],
    )(splat, lo_one, lo_two, own, hi_one, hi_two, wf)

    def swapped(value, bits):
        return lax.ppermute(value, "slab", [(i, i ^ bits) for i in range(slab_count)])

    def slab_terms(value):
        other = swapped(value, 1)
        value = value + other
        bits = 2
        while slab_count // bits > 4:
            value = value + swapped(value, bits)
            bits *= 2
        return [value] + [swapped(value, k) for k in range(bits, slab_count, bits)]

    from_lo = lax.ppermute(up, "slab", ups)
    from_hi = lax.ppermute(dn, "slab", downs)
    pools = slab_terms(pool)
    gw2, e1, wb = call(
        prepare_kernel, 8, 3e9,
        out_shape=[jax.ShapeDtypeStruct((9, 32, 128), f32), big(3), jax.ShapeDtypeStruct((3, 2304, 256), bf16)],
        in_specs=[vmem()] * 5,
        out_specs=[vmem()] * 3,
        scratch_shapes=[pltpu.VMEM((3, 256, 768), f32)],
    )(m3, h2, e2, h1, u)

    ranks = y_count * slab_count
    each = -(-680 // (2 * ranks))
    if each > 8:
        each = -(-each // 8) * 8
    half_rows = each * ranks
    keep, give, scores, pose_loss, dk = call(
        functools.partial(backward_kernel, depth, len(pools)), 18, 1.4e10,
        out_shape=[
            jax.ShapeDtypeStruct((half_rows, 128), f32), jax.ShapeDtypeStruct((half_rows, 128), f32),
            jax.ShapeDtypeStruct((1,), f32), jax.ShapeDtypeStruct((1,), f32),
            jax.ShapeDtypeStruct((4 * OWN, 2048), bf16),
        ],
        in_specs=[smem()] + [vmem()] * (12 + len(pools)),
        out_specs=[vmem(), vmem(), smem(), smem(), vmem()],
        scratch_shapes=[
            pltpu.VMEM((10, BR, 128), bf16), pltpu.VMEM((5, BR, 128), bf16),
            pltpu.VMEM((8, BR, 128), bf16), pltpu.VMEM((4, BR, 128), bf16),
            pltpu.VMEM((6, BR, 128), bf16), pltpu.VMEM((3, BR, 128), bf16),
            pltpu.VMEM((8, R3 * JB, 128), bf16),
            pltpu.VMEM((2, BR, 256), f32), pltpu.VMEM((3, 256, 768), f32),
            pltpu.VMEM((2 * half_rows, 128), f32), pltpu.VMEM((4 * OWN * JB, 128), f32),
        ],
    )(labels, *pools, pool, head, x, ex, h1, e1, h2, m3, from_lo, from_hi, gw2, wb)

    swap = [(0, 1), (1, 0)]
    chip = keep + lax.ppermute(give, "core", swap)
    got = lax.all_to_all(chip.reshape(ranks, each, 128), ("y", "slab"), 0, 0)
    force = call(
        functools.partial(atom_kernel, depth), 12, 1e10,
        out_shape=jax.ShapeDtypeStruct((3, atoms), f32),
        in_specs=[smem(), smem(), vmem(), vmem(), vmem()],
        out_specs=vmem(),
        scratch_shapes=[
            pltpu.VMEM((NXY, atoms), f32), pltpu.VMEM((NXY, atoms), f32), pltpu.VMEM((32, atoms), f32),
            pltpu.VMEM((2048, 256), bf16), pltpu.VMEM((2048, 256), bf16),
        ],
    )(counts, radii, places, atom_types, dk)
    total = jnp.sum(got, axis=0)
    total, force = lax.optimization_barrier((total, force))
    spread_total = jnp.broadcast_to(total[None], (ranks, each, 128))
    gathered = lax.all_to_all(spread_total, ("y", "slab"), 0, 0)
    gathered = gathered.reshape(half_rows, 128)
    gathered_other = lax.ppermute(gathered, "core", swap)
    forces = slab_terms(force)
    force = terms_sum(forces)

    grid = lambda c: jax.ShapeDtypeStruct((27, 32, c), f32)
    stem, one, two, grad_head, atom_grad = call(
        finish_kernel, 6, 1e8,
        out_shape=[grid(w_stem.shape[1]), grid(32), grid(32), jax.ShapeDtypeStruct((1, 32), f32),
                   jax.ShapeDtypeStruct((3, 1, atoms), f32)],
        in_specs=[vmem()] * 3,
        out_specs=[vmem()] * 5,
        scratch_shapes=[pltpu.VMEM((2, half_rows, 128), f32)],
    )(gathered, gathered_other, force)
    shaped = lambda v: v.reshape(3, 3, 3, 32, v.shape[2]).transpose(3, 4, 0, 1, 2)
    return (scores, pose_loss, atom_grad.reshape(1, 3, atoms), shaped(stem), shaped(one), shaped(two),
            grad_head.reshape(32))


def solution(mesh):
    pose_count, slab_count = mesh.shape["pose"], mesh.shape["slab"]
    fine = jax.sharding.Mesh(mesh.devices.reshape(pose_count // 2, 2, slab_count), ("y", "core", "slab"))
    pose = ("y", "core")

    return jax.shard_map(
        local,
        mesh=fine,
        in_specs=(
            P(pose, None, None),
            P(pose, None),
            P(pose),
            P(pose),
            P(pose, None, "slab", None),
            P(),
            P(),
            P(),
            P(),
            P(),
        ),
        out_specs=(P(pose), P(pose), P(pose, None, None), P(), P(), P(), P()),
        check_vma=False,
    )
```

```python
import functools

import jax
import jax.numpy as jnp
from jax import lax
from jax.experimental import pallas as pl
from jax.experimental.pallas import tpu as pltpu
from jax.sharding import PartitionSpec as P


NXY = 64
resolution = 0.375
f32 = jnp.float32
bf16 = jnp.bfloat16

JB = 16
OWN = 32
RD, RS, R2, R3, RM, RG = 38, 37, 36, 35, 34, 33
BR = 41 * JB
CH = 128
NCH = 5
NT = (((1,), (1,)), ((), ()))
NN = (((1,), (0,)), ((), ()))


def dotf(a, b, dims):
    return lax.dot_general(a, b, dims, preferred_element_type=f32)


def lane_block(shape):
    return lax.broadcasted_iota(jnp.int32, shape, 1) // 32


def spread(block, turn):
    if turn == 1:
        return block
    out = pltpu.roll(block, ((turn - 1) * 32) % 128, 1)
    lanes = lane_block(block.shape)
    if turn == 0:
        return jnp.where(lanes == 3, 0.0, out)
    if turn == 3:
        return jnp.where(lanes == 0, 0.0, out)
    return out


def one_block(block, source, target):
    out = pltpu.roll(block, ((target - source) * 32) % 128, 1)
    return jnp.where(lane_block(block.shape) == target, out, 0.0)


def build_forward(u_ref, conv, flip, w_ref):
    zero = jnp.zeros((32, 128), bf16)

    def body(f, carry):
        fe = jnp.where(flip == 0, f, 2 - f)
        at_f = pl.multiple_of(f * 768, 128)
        us = [u_ref[conv * 9 + e * 3 + fe] for e in range(3)]
        for jo in range(4):
            rows = [pl.ds(p * 128 + jo * 32, 32) for p in range(2)]
            for e in range(3):
                main = spread(us[e], jo).astype(bf16)
                for p in range(2):
                    w_ref[rows[p], pl.ds(at_f + (p + e) * 128, 128)] = main
            w_ref[rows[0], pl.ds(at_f + 3 * 128, 128)] = zero
            w_ref[rows[1], pl.ds(at_f, 128)] = zero
            for p in range(2):
                for half in range(2):
                    edge = zero
                    if jo in (0, 3):
                        parts = []
                        for q in (2 * half, 2 * half + 1):
                            if 0 <= q - p <= 2:
                                at = 2 * (q % 2)
                                parts.append(one_block(us[q - p], 0, at) if jo == 0 else one_block(us[q - p], 2, at + 1))
                        edge = functools.reduce(jnp.add, parts).astype(bf16)
                    w_ref[rows[p], pl.ds(at_f + 512 + half * 128, 128)] = edge
        return carry

    lax.fori_loop(0, 3, body, 0)


def build_backward(u_ref, conv, flip, w_ref):
    zero = jnp.zeros((32, 128), bf16)

    def body(f, carry):
        fe = jnp.where(flip == 0, 2 - f, f)
        at_f = pl.multiple_of(f * 768, 128)
        for e in range(3):
            u = u_ref[conv * 9 + (2 - e) * 3 + fe]
            tiles = [spread(u, jc).astype(bf16) for jc in range(4)]
            tiles += [one_block(u, 2, 0).astype(bf16), one_block(u, 0, 3).astype(bf16)]
            for p in range(2):
                q = p + e
                lanes = pl.ds(p * 128, 128)
                for jc in range(6):
                    at = q * 128 + jc * 32 if jc < 4 else 512 + q * 64 + (jc - 4) * 32
                    w_ref[pl.ds(at_f + at, 32), lanes] = tiles[jc]
        for p, q in ((0, 3), (1, 0)):
            lanes = pl.ds(p * 128, 128)
            for jc in range(6):
                at = q * 128 + jc * 32 if jc < 4 else 512 + q * 64 + (jc - 4) * 32
                w_ref[pl.ds(at_f + at, 32), lanes] = zero
        return carry

    lax.fori_loop(0, 3, body, 0)


def edges(a, b):
    n = a.shape[0]
    lanes = lane_block((n, 128))
    mixed = jnp.where(lanes < 2, pltpu.roll(a, 32, 1), pltpu.roll(b, 96, 1))
    down = pltpu.roll(mixed, 1, 0)
    up = pltpu.roll(mixed, n - 1, 0)
    jb = lax.broadcasted_iota(jnp.int32, (n, 128), 0) % JB
    low = jnp.where(jb == 0, 0.0, down)
    high = jnp.where(jb == JB - 1, 0.0, up)
    return jnp.where(lanes % 2 == 0, low, high)


def patch(x_ref, e_ref, plane, pair, f, n):
    sl = pl.ds(f * JB, n)
    return [x_ref[plane + k, sl, :] for k in range(4)] + [e_ref[pair + k, sl, :] for k in range(2)]


def conv_pair(x_ref, e_ref, plane, pair, rows, w_ref, acc_ref, dims):
    n = rows * JB
    lhs = jnp.concatenate([p for f in range(3) for p in patch(x_ref, e_ref, plane, pair, f, n)], axis=1)
    acc_ref[pl.ds(0, n), :] = dotf(lhs, w_ref[...], dims)


def put_pair(main_ref, e_ref, plane, pair, at, va, vb):
    main_ref[plane, pl.ds(at, va.shape[0]), :] = va.astype(bf16)
    main_ref[plane + 1, pl.ds(at, va.shape[0]), :] = vb.astype(bf16)
    if e_ref is not None:
        e_ref[pair, pl.ds(at, va.shape[0]), :] = edges(va, vb).astype(bf16)


def rounded(v):
    return v.astype(bf16).astype(f32)


def clear_pad(ref):
    for k in range(ref.shape[0]):
        ref[k, pl.ds(0, JB), :] = jnp.zeros((JB, 128), ref.dtype)


WIN = 40 * NXY


def pack_planes(h, source, put):
    row = lax.broadcasted_iota(jnp.int32, (256, 256), 0)
    col = lax.broadcasted_iota(jnp.int32, (256, 256), 1)
    mask = jnp.where((row // 32) % 4 == col % 4, 1.0, 0.0).astype(bf16)
    srow = lax.broadcasted_iota(jnp.int32, (64, 256), 0)
    scol = lax.broadcasted_iota(jnp.int32, (64, 256), 1)
    a = srow // JB
    a = jnp.where(h == 0, a, 3 - a)
    pick = jnp.where((srow % JB == (scol // 4) % JB) & (scol // NXY == a), 1.0, 0.0).astype(bf16)
    for ch in range(10):
        at = pl.multiple_of(jnp.where(h == 0, ch, 9 - ch) * 256, 256)
        x0, x1 = source(at)
        wide = jnp.concatenate([x0] * 4 + [x1] * 4, axis=0) * mask
        out = dotf(pick, wide, NT).astype(bf16)
        n = 64 if ch < 9 else 32
        for p in range(2):
            put(p, pl.ds(ch * 64, n), out[:n, p * 128 : (p + 1) * 128])


def widen(raw_ref, wide_ref, sl):
    for p in range(2):
        wide_ref[p, pl.ds(16, 16), :] = jnp.zeros((16, WIN), bf16)
        wide_ref[p, pl.ds(0, raw_ref.shape[1]), :] = raw_ref[p, :, sl]

    def source(at):
        return [wide_ref[p, :, pl.ds(at, 256)] for p in range(2)]

    return source


def pack_own_kernel(raw_ref, low_ref, high_ref, wide_ref):
    h = place()[1]
    base = pl.multiple_of(jnp.where(h == 0, 0, NXY * NXY - WIN), 256)

    def put(p, sl, val):
        (low_ref, high_ref)[p][sl, :] = val

    pack_planes(h, widen(raw_ref, wide_ref, pl.ds(base, WIN)), put)


def pack_kernel(raw_ref, low_ref, high_ref, own_ref, up_ref, dn_ref, wide_ref):
    h = place()[1]

    def put(p, sl, val):
        own_ref[2 * (1 - h) + p, sl, :] = val

    pack_planes(h, widen(raw_ref, wide_ref, pl.ds(0, WIN)), put)
    own_ref[2 * h] = low_ref[...]
    own_ref[2 * h + 1] = high_ref[...]
    for k in range(2):
        up_ref[k] = own_ref[2 - h + k]
        dn_ref[k] = own_ref[1 - h + k]


def weights_kernel(stem_ref, one_ref, two_ref, wf_ref, u_ref):
    flip = place()[1]
    for conv, ref in enumerate((stem_ref, one_ref, two_ref)):
        channels = ref.shape[2]
        blank = jnp.zeros((32, 128 - channels), f32)
        for k in range(9):
            tile = jnp.zeros((32, 128), f32)
            for g in range(3):
                block = jnp.concatenate([ref[3 * k + g].astype(f32), blank], axis=1)
                tile = tile + (pltpu.roll(block, 32 * g, 1) if g else block)
            u_ref[conv * 9 + k] = tile
        build_forward(u_ref, conv, flip, wf_ref.at[conv])


def atom_terms(radii, types):
    radius = jnp.zeros(types.shape, f32)
    for c in range(radii.shape[0]):
        radius = radius + jnp.where(types == c, radii[c], 0.0)
    return 1.0 / (radius * radius)


def centre_rows(n, first, step, half):
    row = lax.broadcasted_iota(jnp.int32, (n, 1), 0)
    return ((first + step * row).astype(f32) + 0.5 - half) * resolution


def bump(centre, place, inv_sq):
    offset = centre - place
    return jnp.exp(-2.0 * offset * offset * inv_sq), offset


def first_row(half):
    return jnp.where(half == 0, 0, NXY - 1), jnp.where(half == 0, 1, -1)


def splat_kernel(depth, count, radii, coords_ref, types_ref, out_ref, z_ref, gy_ref, live_ref, y_ref):
    atoms = types_ref.shape[1]
    types = types_ref[...]
    inv_sq = atom_terms(radii, types)
    group, half = place()
    top, step = first_row(half)
    gx = bump(centre_rows(40, top, step, 0.5 * NXY), coords_ref[0], inv_sq)[0]
    gz = bump(centre_rows(16, 4 * group - 3, 1, 0.5 * depth), coords_ref[2], inv_sq)[0]
    for q in range(10):
        z_ref[pl.ds(q * 40, 40), :] = (gz[q : q + 1, :] * gx).astype(bf16)
    gy_ref[...] = bump(centre_rows(NXY, 0, 1, 0.5 * NXY), coords_ref[1], inv_sq)[0]
    kind = lax.broadcasted_iota(jnp.int32, (32, atoms), 0)
    slot = lax.broadcasted_iota(jnp.int32, (32, atoms), 1)
    live_ref[...] = jnp.where((types == kind) & (slot < count[0]), 1.0, 0.0)

    def body(step8, carry):
        for t in range(8):
            y = gy_ref[pl.ds(step8 * 8 + t, 1), :]
            y_ref[pl.ds(t * 32, 32), :] = (live_ref[...] * y).astype(bf16)
        out = dotf(z_ref[...], y_ref[...], NT)
        out_ref[pl.ds(2 * step8, 400, stride=JB), :] = out[:, :128]
        out_ref[pl.ds(2 * step8 + 1, 400, stride=JB), :] = out[:, 128:]
        return carry

    lax.fori_loop(0, 8, body, 0)


def forward_kernel(
    depth, splat_ref, lo_one, lo_two, own_ref, hi_one, hi_two, w_ref,
    x_ref, ex_ref, h1_ref, h2_ref, e2_ref, m3_ref, up_ref, dn_ref, pool_ref,
    accs_ref, rim_ref, e1_ref,
):
    group, half = place()
    first = 4 * group - 3
    for k, (one, two) in enumerate(((lo_one, lo_two), (hi_one, hi_two))):
        rim_ref[k, 2 * half] = one[...]
        rim_ref[k, 1 - half] = two[0]
        rim_ref[k, 2 - half] = two[1]
    for ref in (x_ref, ex_ref, h1_ref, e1_ref, h2_ref, e2_ref):
        clear_pad(ref)

    def inside(q):
        z = first + q
        return jnp.where((z >= 0) & (z < depth), 1.0, 0.0)

    def kept(acc, q):
        parts = acc[:, :128], acc[:, 128:]
        return [v if 3 <= q + k < 7 else v * inside(q + k) for k, v in enumerate(parts)]

    def receptor(q, sl):
        if q < 3:
            return rim_ref[0, q, sl, :]
        if q < 7:
            return own_ref[q - 3, sl, :]
        return rim_ref[1, q - 7, sl, :]

    def density(m):
        for c in range(4):
            sl = pl.ds(c * 160, 160 if c < 3 else 128)
            n = 160 if c < 3 else 128
            vals = []
            for q in (2 * m, 2 * m + 1):
                v = splat_ref[pl.ds(q * 640 + c * 160, n), :] + receptor(q, sl).astype(f32)
                vals.append(v if 3 <= q < 7 else v * inside(q))
            put_pair(x_ref, ex_ref, 2 * m, m, JB + c * 160, *vals)

    def stem(m, acc_ref):
        conv_pair(x_ref, ex_ref, 2 * m, m, RS, w_ref.at[0], acc_ref, NT)
        for c in range(NCH):
            acc = jnp.maximum(acc_ref[pl.ds(c * CH, CH), :], 0.0)
            put_pair(h1_ref, e1_ref, 2 * m, m, JB + c * CH, *kept(acc, 2 * m + 1))


    def second(m, acc_ref):
        conv_pair(h1_ref, e1_ref, 2 * m, m, R2, w_ref.at[1], acc_ref, NT)
        for c in range(NCH):
            acc = jnp.maximum(acc_ref[pl.ds(c * CH, CH), :], 0.0)
            put_pair(h2_ref, e2_ref, 2 * m, m, JB + c * CH, *kept(acc, 2 * m + 2))


    def third(m, acc_ref):
        pool = jnp.zeros((1, 128), f32)
        conv_pair(h2_ref, e2_ref, 2 * m, m, R3, w_ref.at[2], acc_ref, NT)
        for c in range(7):
            sl = pl.ds(c * 80, 80)
            src = pl.ds(JB + c * 80, 80)
            for k in range(2):
                keep = h1_ref[2 * m + 2 + k, src, :].astype(f32)
                summed = keep + acc_ref[sl, pl.ds(128 * k, 128)]
                top = jnp.maximum(summed, 0.0)
                if (c + 1) * 80 > OWN * JB:
                    row = lax.broadcasted_iota(jnp.int32, (80, 128), 0) + c * 80
                    top = jnp.where(row < OWN * JB, top, 0.0)
                pool = pool + jnp.sum(top, axis=0, keepdims=True)
                m3_ref[2 * m + k, sl, :] = jnp.where(summed > 0.0, 1.0, 0.0).astype(bf16)
        return pool

    steps = iter(range(9))
    turn = lambda: accs_ref.at[next(steps) % 2]
    for m in range(3):
        density(m)
    stem(0, turn())
    density(3)
    stem(1, turn())
    density(4)
    stem(2, turn())
    second(0, turn())
    stem(3, turn())
    second(1, turn())
    pool = third(0, turn())
    second(2, turn())
    pool = pool + third(1, turn())
    pool = pool + pltpu.roll(pool, 64, 1)
    pool = pool + pltpu.roll(pool, 32, 1)
    pool_ref[...] = jnp.broadcast_to(pool, pool_ref.shape)
    for k in range(3):
        up_ref[k] = m3_ref[k + 1]
        dn_ref[k] = m3_ref[k]
    up_ref[3] = h2_ref[3, pl.ds(JB, R3 * JB), :]
    dn_ref[3] = h2_ref[2, pl.ds(JB, R3 * JB), :]


def weight_grad(x_ref, e_ref, plane, pair, grads, g_ref, first):
    ut = jnp.transpose(grads).astype(bf16)
    for f in range(3):
        rhs = jnp.concatenate(patch(x_ref, e_ref, plane, pair, f, OWN * JB), axis=1)
        part = dotf(ut, rhs, NN)
        g_ref[f] = part if first else g_ref[f] + part


def extract(g_ref, flip, scale, put):
    lanes = lane_block((32, 128))

    def body(f, carry):
        fe = jnp.where(flip == 0, f, 2 - f)
        for e in range(3):
            total = jnp.zeros((32, 128), f32)
            for p in range(2):
                q = p + e
                for jo in range(4):
                    rows = pl.ds(p * 128 + jo * 32, 32)
                    block = g_ref[f, rows, pl.ds(q * 128, 128)]
                    if jo != 1:
                        block = pltpu.roll(block, ((1 - jo) * 32) % 128, 1)
                    if jo == 0:
                        block = jnp.where((lanes == 1) | (lanes == 2), block, 0.0)
                    elif jo == 3:
                        block = jnp.where(lanes < 2, block, 0.0)
                    else:
                        block = jnp.where(lanes < 3, block, 0.0)
                    total = total + block
                    if jo in (0, 3):
                        side = g_ref[f, rows, pl.ds(512 + (q // 2) * 128, 128)]
                        at = 2 * (q % 2)
                        total = total + (one_block(side, at, 0) if jo == 0 else one_block(side, at + 1, 2))
            put(e * 3 + fe, total * scale)
        return carry

    for f in range(3):
        body(f, 0)


def prepare_kernel(m3_ref, h2_ref, e2_ref, h1_ref, u_ref, gw_ref, e1_ref, wb_ref, g_ref):
    flip = place()[1]
    for conv in range(3):
        build_backward(u_ref, conv, flip, wb_ref.at[conv])
    clear_pad(e1_ref)
    for m in range(3):
        for c in range(5):
            sl = pl.ds(JB + c * CH, CH)
            sides = [h1_ref[2 * m + 1 + k, sl, :].astype(f32) for k in range(2)]
            e1_ref[m, sl, :] = edges(*sides).astype(bf16)
    rows = pl.ds(0, OWN * JB)
    for m in range(2):
        grads = jnp.concatenate([m3_ref[2 * m, rows, :], m3_ref[2 * m + 1, rows, :]], axis=1)
        weight_grad(h2_ref, e2_ref, 2 * m, m, grads, g_ref, m == 0)

    def put(k, val):
        gw_ref[k] = val

    extract(g_ref, flip, 1.0, put)


def backward_kernel(
    depth, terms, label, *refs,
):
    pool_refs, refs = refs[:terms], refs[terms:]
    mine_ref, head_ref, x_ref, ex_ref, h1_ref, e1_ref, h2_ref, m3_ref, lo_ref, hi_ref, gw2_ref, w_ref = refs[:12]
    keep_ref, give_ref, score_ref, loss_ref, dk_ref = refs[12:17]
    t_ref, et_ref, mg_ref, em_ref, sg_ref, es_ref, hm_ref, accs_ref, g_ref, flat_ref, dg_ref = refs[17:]
    flip = place()[1]
    scale = 1.0 / (depth * NXY * NXY)
    head = head_ref[...]
    pooled = terms_sum([ref[0:1, :] for ref in pool_refs]) * scale
    lane = lax.broadcasted_iota(jnp.int32, (1, 128), 1)
    score = jnp.sum(jnp.where(lane < 32, pooled * head, 0.0), axis=1, keepdims=True)
    sign = (2 * label[0] - 1).astype(f32)
    logit = -sign * score
    score_grad = -sign / (1.0 + jnp.exp(-logit))
    loss = jnp.maximum(logit, 0.0) + jnp.log1p(jnp.exp(-jnp.abs(logit)))
    score_ref[0] = jnp.sum(score)
    loss_ref[0] = jnp.sum(loss)
    tone = rounded(score_grad * head)

    half_rows = keep_ref.shape[0]
    lanes = lane_block((32, 128))
    eye = lax.broadcasted_iota(jnp.int32, (32, 128), 0) == lax.broadcasted_iota(jnp.int32, (32, 128), 1)
    tall = jnp.sum(jnp.where(eye, tone, 0.0), axis=1, keepdims=True) * scale
    for k in range(6):
        tile = gw2_ref[k] * tall
        for g in range(3):
            flat_ref[pl.ds((3 * k + g) * 32, 32), :] = one_block(tile, g, 3)
    for k in range(3):
        flat_ref[pl.ds((18 + k) * 32, 32), :] = gw2_ref[6 + k] * tall
    tail = 2 * half_rows - 672
    flat_ref[pl.ds(672, tail), :] = jnp.where(
        lax.broadcasted_iota(jnp.int32, (tail, 128), 0) == 0, score_grad * mine_ref[0:1, :] * scale, 0.0
    )

    def put_rows(conv):
        def put(k, val):
            rows = pl.ds(pl.multiple_of((conv * 9 + k) * 32, 32), 32)
            flat_ref[rows, :] = jnp.where(lanes < 3, val, flat_ref[rows, :])

        return put

    for ref in (t_ref, et_ref, mg_ref, em_ref, sg_ref, es_ref):
        clear_pad(ref)
    mask_of = lambda q: (lo_ref.at[q] if q < 3 else m3_ref.at[q - 3] if q < 7 else hi_ref.at[q - 7])

    def top(m):
        for c in range(5):
            sl = pl.ds(c * 112, 112)
            vals = [jnp.where(mask_of(q)[sl, :].astype(f32) > 0.0, tone, 0.0) for q in (2 * m, 2 * m + 1)]
            put_pair(t_ref, et_ref, 2 * m, m, JB + c * 112, *vals)

    hm_ref[0] = lo_ref[3]
    hm_ref[7] = hi_ref[3]
    for k in range(6):
        hm_ref[k + 1] = h2_ref[k, pl.ds(JB, R3 * JB), :]

    own_rows = pl.ds(JB, OWN * JB)

    def mid(m, acc_ref):
        conv_pair(t_ref, et_ref, 2 * m, m, RM, w_ref.at[2], acc_ref, NN)
        for c in range(NCH):
            sl = pl.ds(c * 112, 112)
            vals = [
                jnp.where(hm_ref[2 * m + k, sl, :].astype(f32) > 0.0, acc_ref[sl, pl.ds(128 * k, 128)], 0.0)
                for k in range(2)
            ]
            put_pair(mg_ref, em_ref, 2 * m, m, JB + c * 112, *vals)


    def grad_one(m):
        grads = jnp.concatenate([mg_ref[2 + 2 * m, own_rows, :], mg_ref[3 + 2 * m, own_rows, :]], axis=1)
        weight_grad(h1_ref, e1_ref, 1 + 2 * m, m, grads, g_ref.at[1], m == 0)

    def low(m, acc_ref):
        conv_pair(mg_ref, em_ref, 2 * m, m, RG, w_ref.at[1], acc_ref, NN)
        for c in range(NCH):
            sl = pl.ds(c * 112, 112)
            src = pl.ds(JB + c * 112, 112)
            vals = []
            for k in range(2):
                back = t_ref[2 * m + 2 + k, src, :].astype(f32) + acc_ref[sl, pl.ds(128 * k, 128)]
                vals.append(jnp.where(h1_ref[2 * m + 1 + k, src, :].astype(f32) > 0.0, back, 0.0))
            put_pair(sg_ref, es_ref, 2 * m, m, JB + c * 112, *vals)


    def grad_stem(m):
        grads = jnp.concatenate([sg_ref[1 + 2 * m, own_rows, :], sg_ref[2 + 2 * m, own_rows, :]], axis=1)
        weight_grad(x_ref, ex_ref, 2 + 2 * m, 1 + m, grads, g_ref.at[0], m == 0)

    def last(m, acc_ref):
        conv_pair(sg_ref, es_ref, 2 * m, m, OWN, w_ref.at[0], acc_ref, NN)
        for k in range(2):
            at = pl.ds(pl.multiple_of((2 * m + k) * OWN * JB, 16), OWN * JB)
            dg_ref[at, :] = acc_ref[pl.ds(0, OWN * JB), pl.ds(128 * k, 128)]

    steps = iter(range(9))
    turn = lambda: accs_ref.at[next(steps) % 2]
    for m in range(3):
        top(m)
    mid(0, turn())
    top(3)
    mid(1, turn())
    top(4)
    mid(2, turn())
    grad_one(0)
    low(0, turn())
    mid(3, turn())
    grad_one(1)
    low(1, turn())
    low(2, turn())
    extract(g_ref.at[1], flip, scale, put_rows(1))
    grad_stem(0)
    last(0, turn())
    grad_stem(1)
    extract(g_ref.at[0], flip, scale, put_rows(0))
    last(1, turn())
    for jb in range(JB):
        dk_ref[:, pl.ds(jb * 128, 128)] = dg_ref[pl.ds(jb, 4 * OWN, stride=JB), :].astype(bf16)

    core = lax.axis_index("core")
    keep_ref[...] = flat_ref[pl.ds(pl.multiple_of(core * half_rows, 16), half_rows), :]
    give_ref[...] = flat_ref[pl.ds(pl.multiple_of((1 - core) * half_rows, 16), half_rows), :]


def atom_kernel(depth, count, radii, coords_ref, types_ref, dk_ref, force_ref, gy_ref, sy_ref, live_ref, y_ref, dy_ref):
    types = types_ref[...]
    inv_sq = atom_terms(radii, types)
    atoms = types.shape[1]
    gy, off = bump(centre_rows(NXY, 0, 1, 0.5 * NXY), coords_ref[1], inv_sq)
    gy_ref[...] = gy
    sy_ref[...] = 4.0 * off * inv_sq * gy
    kind = lax.broadcasted_iota(jnp.int32, (32, atoms), 0)
    slot = lax.broadcasted_iota(jnp.int32, (32, atoms), 1)
    live_ref[...] = jnp.where((types == kind) & (slot < count[0]), 1.0, 0.0)
    group, half = place()
    top, step = first_row(half)
    wide = 256
    for b in range(atoms // wide):
        sl = pl.ds(b * wide, wide)

        def table(j, carry):
            live = live_ref[:, sl]
            at = pl.ds(pl.multiple_of(j * 32, 32), 32)
            y_ref[at, :] = (live * gy_ref[pl.ds(j, 1), sl]).astype(bf16)
            dy_ref[at, :] = (live * sy_ref[pl.ds(j, 1), sl]).astype(bf16)
            return carry

        lax.fori_loop(0, NXY, table, 0, unroll=4)
        plain = dotf(dk_ref[...], y_ref[...], NN)
        slope = dotf(dk_ref[...], dy_ref[...], NN)
        inv = inv_sq[:, b * wide : (b + 1) * wide]
        gx, off_x = bump(centre_rows(OWN, top, step, 0.5 * NXY), coords_ref[0, :, sl], inv)
        dgx = 4.0 * off_x * inv * gx
        gz, off_z = bump(centre_rows(8, 4 * group, 1, 0.5 * depth), coords_ref[2, :, sl], inv)
        dgz = 4.0 * off_z * inv * gz
        fx = jnp.zeros((1, wide), f32)
        fy = jnp.zeros((1, wide), f32)
        fz = jnp.zeros((1, wide), f32)
        for k in range(4):
            pk = plain[k * OWN : (k + 1) * OWN, :]
            sk = slope[k * OWN : (k + 1) * OWN, :]
            fx = fx + gz[k : k + 1, :] * jnp.sum(pk * dgx, axis=0, keepdims=True)
            fy = fy + gz[k : k + 1, :] * jnp.sum(sk * gx, axis=0, keepdims=True)
            fz = fz + dgz[k : k + 1, :] * jnp.sum(pk * gx, axis=0, keepdims=True)
        force_ref[0:1, sl] = fx
        force_ref[1:2, sl] = fy
        force_ref[2:3, sl] = fz


def terms_sum(terms):
    if len(terms) == 1:
        return terms[0]
    half = len(terms) // 2
    return terms_sum([a + b for a, b in zip(terms[:half], terms[half:])])


def place():
    s = lax.axis_index("slab")
    return s // 2, s % 2


def smem():
    return pl.BlockSpec(memory_space=pltpu.SMEM)


def vmem():
    return pl.BlockSpec(memory_space=pltpu.VMEM)


def finish_kernel(mine_ref, other_ref, sum_ref, stem_ref, one_ref, two_ref, head_ref, force_ref, both_ref):
    core = lax.axis_index("core")
    both_ref[core] = mine_ref[...]
    both_ref[1 - core] = other_ref[...]
    half_rows = mine_ref.shape[0]

    def tile(t):
        return both_ref[t * 32 // half_rows, pl.ds(t * 32 % half_rows, 32), :]

    for t in range(27):
        conv, k = divmod(t, 9)
        ref = (stem_ref, one_ref, two_ref)[conv]
        for g in range(3):
            if conv < 2:
                block, at = tile(t), g
            elif k < 6:
                block, at = tile(3 * k + g), 3
            else:
                block, at = tile(12 + k), g
            val = pltpu.roll(block, 128 - 32 * at, 1) if at else block
            ref[3 * k + g] = val[:, : ref.shape[2]]
    head_ref[...] = both_ref[672 // half_rows, pl.ds(672 % half_rows, 8), :][:1, :32]
    for k in range(3):
        force_ref[k] = sum_ref[k : k + 1, :]


def call(kernel, limit, flops, **kwargs):
    return pl.pallas_call(
        kernel,
        compiler_params=pltpu.CompilerParams(vmem_limit_bytes=limit << 20),
        cost_estimate=pl.CostEstimate(flops=int(flops), bytes_accessed=4_000_000, transcendentals=0),
        **kwargs,
    )


def local(coords, atom_types, counts, labels, receptor, radii, w_stem, w_one, w_two, w_head):
    slab_count = lax.axis_size("slab")
    y_count = lax.axis_size("y")
    atoms = coords.shape[2]
    half = lax.axis_index("slab") % 2
    depth = receptor.shape[2] * slab_count
    bh = (RD * JB, 128)
    places = coords.reshape(3, 1, atoms)

    raw = jnp.transpose(receptor[0], (1, 0, 2))
    theirs = lax.dynamic_slice_in_dim(raw, jnp.where(half == 1, 0, NXY * NXY - WIN), WIN, 2)
    other = lax.ppermute(theirs, "slab", [(i, i ^ 1) for i in range(slab_count)])
    low, high = call(
        pack_own_kernel, 6, 2e9,
        out_shape=[jax.ShapeDtypeStruct(bh, bf16)] * 2,
        in_specs=[vmem()],
        out_specs=[vmem()] * 2,
        scratch_shapes=[pltpu.VMEM((2, 32, WIN), bf16)],
    )(raw)
    offsets = lambda w: jnp.transpose(w, (2, 3, 4, 0, 1)).reshape(27, 32, w.shape[1])
    head = jnp.tile(w_head, 4)[None, :]
    ups = [(i, i + 2) for i in range(slab_count - 2)]
    downs = [(i + 2, i) for i in range(slab_count - 2)]
    lo_one = lax.ppermute(high, "slab", ups)
    hi_one = lax.ppermute(low, "slab", downs)
    other, head = lax.optimization_barrier((other, head))
    own, own_up, own_dn = call(
        pack_kernel, 6, 2e9,
        out_shape=[jax.ShapeDtypeStruct((n,) + bh, bf16) for n in (4, 2, 2)],
        in_specs=[vmem()] * 3,
        out_specs=[vmem()] * 3,
        scratch_shapes=[pltpu.VMEM((2, 32, WIN), bf16)],
    )(other, low, high)
    lo_two = lax.ppermute(own_up, "slab", ups)
    hi_two = lax.ppermute(own_dn, "slab", downs)

    own, w_stem, w_one, w_two = lax.optimization_barrier((own, w_stem, w_one, w_two))
    wf, u = call(
        weights_kernel, 6, 3e9,
        out_shape=[jax.ShapeDtypeStruct((3, 256, 2304), bf16), jax.ShapeDtypeStruct((27, 32, 128), f32)],
        in_specs=[vmem()] * 3,
        out_specs=[vmem()] * 2,
    )(offsets(w_stem), offsets(w_one), offsets(w_two))
    splat = call(
        functools.partial(splat_kernel, depth), 10, 8e9,
        out_shape=jax.ShapeDtypeStruct((6400, 128), f32),
        in_specs=[smem(), smem(), vmem(), vmem()],
        out_specs=vmem(),
        scratch_shapes=[
            pltpu.VMEM((400, atoms), bf16),
            pltpu.VMEM((NXY, atoms), f32),
            pltpu.VMEM((32, atoms), f32),
            pltpu.VMEM((256, atoms), bf16),
        ],
    )(counts, radii, places, atom_types)

    big = lambda n: jax.ShapeDtypeStruct((n, BR, 128), bf16)
    thin = lambda n: jax.ShapeDtypeStruct((n, R3 * JB, 128), bf16)
    x, ex, h1, h2, e2, m3, up, dn, pool = call(
        functools.partial(forward_kernel, depth), 8, 1.4e10,
        out_shape=[big(10), big(5), big(8), big(6), big(3), thin(4), thin(4), thin(4),
                   jax.ShapeDtypeStruct((8, 128), f32)],
        in_specs=[vmem()] * 7,
        out_specs=[vmem()] * 9,
        scratch_shapes=[
            pltpu.VMEM((2, BR, 256), f32), pltpu.VMEM((2, 3) + bh, bf16), pltpu.VMEM((4, BR, 128), bf16),
        ],
    )(splat, lo_one, lo_two, own, hi_one, hi_two, wf)

    def swapped(value, bits):
        return lax.ppermute(value, "slab", [(i, i ^ bits) for i in range(slab_count)])

    def slab_terms(value):
        other = swapped(value, 1)
        value = value + other
        bits = 2
        while slab_count // bits > 4:
            value = value + swapped(value, bits)
            bits *= 2
        return [value] + [swapped(value, k) for k in range(bits, slab_count, bits)]

    from_lo = lax.ppermute(up, "slab", ups)
    from_hi = lax.ppermute(dn, "slab", downs)
    pools = slab_terms(pool)
    gw2, e1, wb = call(
        prepare_kernel, 8, 3e9,
        out_shape=[jax.ShapeDtypeStruct((9, 32, 128), f32), big(3), jax.ShapeDtypeStruct((3, 2304, 256), bf16)],
        in_specs=[vmem()] * 5,
        out_specs=[vmem()] * 3,
        scratch_shapes=[pltpu.VMEM((3, 256, 768), f32)],
    )(m3, h2, e2, h1, u)

    ranks = y_count * slab_count
    each = -(-680 // (2 * ranks))
    if each > 8:
        each = -(-each // 8) * 8
    half_rows = each * ranks
    keep, give, scores, pose_loss, dk = call(
        functools.partial(backward_kernel, depth, len(pools)), 22, 1.4e10,
        out_shape=[
            jax.ShapeDtypeStruct((half_rows, 128), f32), jax.ShapeDtypeStruct((half_rows, 128), f32),
            jax.ShapeDtypeStruct((1,), f32), jax.ShapeDtypeStruct((1,), f32),
            jax.ShapeDtypeStruct((4 * OWN, 2048), bf16),
        ],
        in_specs=[smem()] + [vmem()] * (12 + len(pools)),
        out_specs=[vmem(), vmem(), smem(), smem(), vmem()],
        scratch_shapes=[
            pltpu.VMEM((10, BR, 128), bf16), pltpu.VMEM((5, BR, 128), bf16),
            pltpu.VMEM((8, BR, 128), bf16), pltpu.VMEM((4, BR, 128), bf16),
            pltpu.VMEM((6, BR, 128), bf16), pltpu.VMEM((3, BR, 128), bf16),
            pltpu.VMEM((8, R3 * JB, 128), bf16),
            pltpu.VMEM((2, BR, 256), f32), pltpu.VMEM((2, 3, 256, 768), f32),
            pltpu.VMEM((2 * half_rows, 128), f32), pltpu.VMEM((4 * OWN * JB, 128), f32),
        ],
    )(labels, *pools, pool, head, x, ex, h1, e1, h2, m3, from_lo, from_hi, gw2, wb)

    swap = [(0, 1), (1, 0)]
    chip = keep + lax.ppermute(give, "core", swap)
    got = lax.all_to_all(chip.reshape(ranks, each, 128), ("y", "slab"), 0, 0)
    force = call(
        functools.partial(atom_kernel, depth), 12, 1e10,
        out_shape=jax.ShapeDtypeStruct((3, atoms), f32),
        in_specs=[smem(), smem(), vmem(), vmem(), vmem()],
        out_specs=vmem(),
        scratch_shapes=[
            pltpu.VMEM((NXY, atoms), f32), pltpu.VMEM((NXY, atoms), f32), pltpu.VMEM((32, atoms), f32),
            pltpu.VMEM((2048, 256), bf16), pltpu.VMEM((2048, 256), bf16),
        ],
    )(counts, radii, places, atom_types, dk)
    total = jnp.sum(got, axis=0)
    total, force = lax.optimization_barrier((total, force))
    spread_total = jnp.broadcast_to(total[None], (ranks, each, 128))
    gathered = lax.all_to_all(spread_total, ("y", "slab"), 0, 0)
    gathered = gathered.reshape(half_rows, 128)
    gathered_other = lax.ppermute(gathered, "core", swap)
    forces = slab_terms(force)
    force = terms_sum(forces)

    grid = lambda c: jax.ShapeDtypeStruct((27, 32, c), f32)
    stem, one, two, grad_head, atom_grad = call(
        finish_kernel, 6, 1e8,
        out_shape=[grid(w_stem.shape[1]), grid(32), grid(32), jax.ShapeDtypeStruct((1, 32), f32),
                   jax.ShapeDtypeStruct((3, 1, atoms), f32)],
        in_specs=[vmem()] * 3,
        out_specs=[vmem()] * 5,
        scratch_shapes=[pltpu.VMEM((2, half_rows, 128), f32)],
    )(gathered, gathered_other, force)
    shaped = lambda v: v.reshape(3, 3, 3, 32, v.shape[2]).transpose(3, 4, 0, 1, 2)
    return (scores, pose_loss, atom_grad.reshape(1, 3, atoms), shaped(stem), shaped(one), shaped(two),
            grad_head.reshape(32))


def solution(mesh):
    pose_count, slab_count = mesh.shape["pose"], mesh.shape["slab"]
    fine = jax.sharding.Mesh(mesh.devices.reshape(pose_count // 2, 2, slab_count), ("y", "core", "slab"))
    pose = ("y", "core")

    return jax.shard_map(
        local,
        mesh=fine,
        in_specs=(
            P(pose, None, None),
            P(pose, None),
            P(pose),
            P(pose),
            P(pose, None, "slab", None),
            P(),
            P(),
            P(),
            P(),
            P(),
        ),
        out_specs=(P(pose), P(pose), P(pose, None, None), P(), P(), P(), P()),
        check_vma=False,
    )
```
